256 devices in a mesh: dp: 2 (over y_lo), view: 16 (over x, y_hi, core), head: 8 (over z).
Axes of the slice: x: 4, y: 4 (y_hi: 2, y_lo: 2; y = y_hi * 2 + y_lo), z: 8, core: 2. Of those that a mesh axis runs over, the one named last changes fastest.
Arguments:
- normed: bfloat16 [2, 16, 256, 3072], P('dp', 'view'), may hold values from -6 to 6
- queries: bfloat16 [2, 16, 256, 3072], P('dp', 'view', None, 'head'), may hold values from -180 to 180
- saved_keys: bfloat16 [2, 16, 256, 3072], P('dp', 'view', None, 'head'), may hold values from -4.5 to 4.5
- saved_values: bfloat16 [2, 16, 256, 3072], P('dp', 'view', None, 'head'), may hold values from -6 to 6
- output_grad: bfloat16 [2, 16, 256, 3072], P('dp', 'view', None, 'head'), may hold values from -200 to 200
- view_links: int32 [16, 2], P('view'), may hold values from -1 to 15, as said below
- query_weight: bfloat16 [3072, 3072], P(('dp', 'view'), 'head'), may hold values from -0.109375 to 0.109375
- key_weight: bfloat16 [3072, 3072], P(('dp', 'view'), 'head'), may hold values from -0.109375 to 0.109375
- value_weight: bfloat16 [3072, 3072], P(('dp', 'view'), 'head'), may hold values from -0.109375 to 0.109375
Outputs:
- input_grad: bfloat16 [2, 16, 256, 3072], P('dp', 'view', None, 'head')
- grad_query: float32 [3072, 3072], P(('dp', 'view'), 'head')
- grad_key: float32 [3072, 3072], P(('dp', 'view'), 'head')
- grad_value: float32 [3072, 3072], P(('dp', 'view'), 'head')
The draws below stay inside these ranges and needn't reach their ends.
Inputs may be any that keep to these rules, and one draw needn't show every extreme that they name: `view_links`: row v holds (v - 1) mod 16 or -1 and then (v + 1) mod 16 or -1; -1 marks a link that view v does not attend.
All inputs are finite; a program needn't handle non-finite values.
Results may differ from the reference program's by a relative error of at most 0.0057.
Values may be sent and summed in bfloat16 or wider, within the bound.
A program may use at most 128 MiB of HBM per device.

```python
import jax
import jax.numpy as jnp
from jax import lax

D = 3072
HEADS = 24
HD = 128
S = 256
VIEWS = 16
PROMPTS = 2


def clipped_normal(key, salt):
    values = jax.random.normal(jax.random.fold_in(key, salt), (PROMPTS, VIEWS, S, HEADS * HD), jnp.float32)
    return jnp.clip(values, -4.5, 4.5)


def draw_saved_keys(key, part):
    key_rows = clipped_normal(key, 3)
    return key_rows.astype(jnp.bfloat16)


def draw_queries(key, part):
    query_rows = clipped_normal(key, 4)
    return query_rows.astype(jnp.bfloat16)


def draw_view_links(key, part):
    numbers = jnp.arange(VIEWS, dtype=jnp.int32)
    previous = (numbers - 1) % VIEWS
    following = (numbers + 1) % VIEWS
    kept_link = jax.random.randint(key, (VIEWS, 2), 0, 4) != 0
    kept_link = kept_link.at[0, 0].set(True).at[0, 1].set(True)
    kept_link = kept_link.at[1, 0].set(True).at[1, 1].set(False)
    return jnp.where(kept_link, jnp.stack([previous, following], axis=1), -1).astype(jnp.int32)


def spiked(entries, stream_key, source, target, blocks, factor):
    owner, partner = [(jnp.arange(entries.shape[dim]) // (entries.shape[dim] // blocks)).reshape([-1 if axis == dim else 1 for axis in range(entries.ndim)]) for dim in (source, target)]
    chosen = jax.random.permutation(stream_key, blocks)[partner]
    strong = (owner == chosen) | (owner == (partner + blocks // 2) % blocks)
    return jnp.where(strong, factor * entries, entries)


def block_levels(key, shape, pieces, least, high):
    def one(dim, blocks):
        heights = jax.random.uniform(jax.random.fold_in(jax.random.fold_in(key, 6), dim), (blocks,), jnp.float32, least / len(pieces), high / len(pieces))
        return jnp.repeat(jnp.exp(heights), shape[dim] // blocks).reshape((-1,) + (1,) * (len(shape) - dim - 1))

    loudness = one(*pieces[0])
    for cut in pieces[1:]:
        loudness = loudness * one(*cut)
    return loudness


def centred(stream_key, shape, width, most, shards=(), held_as=jnp.bfloat16):
    entries = width * jax.random.normal(stream_key, shape, jnp.float32)
    if shards:
        entries = entries * block_levels(stream_key, shape, shards, -0.22, 0.18)
    return jnp.clip(entries, -most, most).astype(held_as)


def heavy_noise(own_key, dims, spread, reach, pieces, heavy, held_as=jnp.bfloat16):
    array = spread * jax.random.normal(own_key, dims, jnp.float32)
    if pieces:
        array = array * block_levels(own_key, dims, pieces, -0.22, 0.18)
    return jnp.clip(spiked(array, jax.random.fold_in(own_key, 3), *heavy), -reach, reach).astype(held_as)


def setup_inputs(seed: int = 0) -> dict:
    key_of = jax.random.split(jax.random.key(seed), 10)
    normed = heavy_noise(key_of[0], (PROMPTS, VIEWS, S, D), 1.0, 6.0, ((0, 2), (1, 16)), (1, 3, 16, 2.0))
    queries = draw_queries(jax.random.fold_in(key_of[9], 71), 0)
    saved_keys = draw_saved_keys(jax.random.fold_in(key_of[9], 71), 0)
    saved_values = centred(key_of[3], (PROMPTS, VIEWS, S, HEADS * HD), 1.0, 6.0, ((0, 2), (1, 16), (3, 8)))
    output_grad = centred(key_of[4], (PROMPTS, VIEWS, S, HEADS * HD), 32.0, 200.0, ((0, 2), (1, 16), (3, 8)))
    view_links = draw_view_links(jax.random.fold_in(key_of[9], 71), 0)
    query_weight = centred(key_of[6], (D, HEADS * HD), D ** -0.5, 0.109375, ((0, 32), (1, 8)))
    key_weight = centred(key_of[7], (D, HEADS * HD), D ** -0.5, 0.109375, ((0, 32), (1, 8)))
    value_weight = centred(key_of[8], (D, HEADS * HD), D ** -0.5, 0.109375, ((0, 32), (1, 8)))
    return dict(normed=normed, queries=queries, saved_keys=saved_keys, saved_values=saved_values, output_grad=output_grad, view_links=view_links, query_weight=query_weight, key_weight=key_weight, value_weight=value_weight)


def softmax_rows(scores):
    largest = jnp.max(scores, axis=-1, keepdims=True)
    powers = jnp.exp(scores - largest)
    return powers / jnp.sum(powers, axis=-1, keepdims=True)


def reference(normed, queries, saved_keys, saved_values, output_grad, view_links, query_weight, key_weight, value_weight):
    scaling = HD ** -0.5
    col_count = HEADS * HD
    block_index = jnp.arange(3 * S) // S

    def one_view(view):
        previous = (view - 1) % VIEWS
        following = (view + 1) % VIEWS

        def three_blocks(source):
            return jnp.stack([source[:, previous], source[:, view], source[:, following]], axis=1)

        key_heads = three_blocks(saved_keys).astype(jnp.float32).reshape(PROMPTS, 3 * S, HEADS, HD)
        value_heads = three_blocks(saved_values).astype(jnp.float32).reshape(PROMPTS, 3 * S, HEADS, HD)
        query_heads = queries[:, view].astype(jnp.float32).reshape(PROMPTS, S, HEADS, HD)
        grad_heads = output_grad[:, view].astype(jnp.float32).reshape(PROMPTS, S, HEADS, HD)
        link_flags = view_links[view] >= 0
        usable = jnp.where(block_index == 0, link_flags[0], jnp.where(block_index == 2, link_flags[1], True))
        scores = jnp.einsum("bshd,bthd->bhst", query_heads, key_heads) * scaling
        scores = jnp.where(usable, scores, -1e30)
        attn_probs = softmax_rows(scores)
        probs_half = lax.optimization_barrier(attn_probs.astype(jnp.bfloat16)).astype(jnp.float32)
        prob_grad = jnp.einsum("bshd,bthd->bhst", grad_heads, value_heads)
        row_delta = jnp.sum(attn_probs * prob_grad, axis=-1, keepdims=True)
        score_grad = lax.optimization_barrier((scaling * attn_probs * (prob_grad - row_delta)).astype(jnp.bfloat16)).astype(jnp.float32)
        query_grad = jnp.einsum("bhst,bthd->bshd", score_grad, key_heads).reshape(PROMPTS, S, col_count)
        key_grad = jnp.einsum("bhst,bshd->bthd", score_grad, query_heads).reshape(PROMPTS, 3, S, col_count)
        value_grad = jnp.einsum("bhst,bshd->bthd", probs_half, grad_heads).reshape(PROMPTS, 3, S, col_count)
        return query_grad, key_grad, value_grad

    query_all, key_parts, value_parts = lax.map(one_view, jnp.arange(VIEWS, dtype=jnp.int32))

    def gather_parts(parts):
        return parts[:, :, 1] + jnp.roll(parts[:, :, 0], -1, axis=0) + jnp.roll(parts[:, :, 2], 1, axis=0)

    row_count = PROMPTS * VIEWS * S
    query_half = jnp.moveaxis(query_all, 0, 1).astype(jnp.bfloat16).reshape(row_count, col_count)
    key_half = jnp.moveaxis(gather_parts(key_parts), 0, 1).astype(jnp.bfloat16).reshape(row_count, col_count)
    value_half = jnp.moveaxis(gather_parts(value_parts), 0, 1).astype(jnp.bfloat16).reshape(row_count, col_count)

    running = jnp.dot(query_half, query_weight.T, preferred_element_type=jnp.float32)
    running = running + jnp.dot(key_half, key_weight.T, preferred_element_type=jnp.float32)
    running = running + jnp.dot(value_half, value_weight.T, preferred_element_type=jnp.float32)
    input_grad = running.astype(jnp.bfloat16).reshape(PROMPTS, VIEWS, S, D)

    flat_input = normed.reshape(row_count, D)
    mean_scale = 1.0 / (PROMPTS * VIEWS)
    grad_query = jnp.dot(flat_input.T, query_half, preferred_element_type=jnp.float32) * mean_scale
    grad_key = jnp.dot(flat_input.T, key_half, preferred_element_type=jnp.float32) * mean_scale
    grad_value = jnp.dot(flat_input.T, value_half, preferred_element_type=jnp.float32) * mean_scale
    return (input_grad, grad_query, grad_key, grad_value)
```

```python
import functools

import jax
import jax.numpy as jnp
from jax import lax
from jax.experimental import pallas as pl
from jax.experimental.pallas import tpu as pltpu
from jax.sharding import PartitionSpec as P

HD = 128
MESH = pl.DeviceIdType.MESH
F32 = jnp.float32
BF16 = jnp.bfloat16
NT = (((1,), (1,)), ((), ()))
NN = (((1,), (0,)), ((), ()))
TN = (((0,), (0,)), ((), ()))


def dot(a, b, dims):
    return lax.dot_general(a, b, dims, preferred_element_type=F32)


def kernel(
    links, normed, q_ref, k_ref, v_ref, g_ref, wq, wk, wv,
    dx_out, dq_out, dk_out, dv_out,
    kv, wg, nt, ntp, hown, hpar, own, gs, gr, part, ra1, rra, rb, rb1, rrb, zb, zr,
    ssem, rsem, lsem,
):
    length, cols = q_ref.shape
    heads = cols // HD
    rows = wq.shape[0]
    half = rows // 2
    scaling = HD ** (-0.5)
    dp, vw, z = lax.axis_index("dp"), lax.axis_index("view"), lax.axis_index("head")
    nview, nz = 16, 8
    x = lax.div(vw, 4)
    yh = lax.rem(lax.div(vw, 2), 2)
    c = lax.rem(vw, 2)
    y = yh * 2 + dp

    def at(xx, yy, cc, zz):
        return (lax.rem(yy, 2), xx * 4 + lax.div(yy, 2) * 2 + cc, zz)

    def m(value, n):
        return lax.rem(value + n, n)

    x_up, x_dn, x_far = m(x + 1, 4), m(x - 1, 4), m(x + 2, 4)
    y_up, y_dn = m(y + 1, 4), m(y - 1, 4)
    to_x = {1: at(x_up, y, c, z), -1: at(x_dn, y, c, z)}
    to_y = {1: at(x, y_up, c, z), -1: at(x, y_dn, c, z)}
    to_z = {1: (dp, vw, m(z + 1, nz)), -1: (dp, vw, m(z - 1, nz))}
    to_view = {1: (dp, m(vw + 1, nview), z), -1: (dp, m(vw - 1, nview), z)}
    partner = at(x, y, 1 - c, z)

    started = []

    def send(src, dst, device):
        slot = len(started)
        copy = pltpu.make_async_remote_copy(
            src_ref=src, dst_ref=dst, send_sem=ssem.at[slot], recv_sem=rsem.at[slot],
            device_id=device, device_id_type=MESH,
        )
        copy.start()
        started.append(copy)
        return copy

    barrier = pltpu.get_barrier_semaphore()
    for peers in (to_view, to_x, to_y, to_z):
        for step in (1, -1):
            pl.semaphore_signal(barrier, inc=1, device_id=peers[step], device_id_type=MESH)
    yl = dp
    locals_ = []
    for i, w in enumerate((wq, wk, wv)):
        copy = pltpu.make_async_copy(
            w, wg.at[x, yl, yh, c, :, pl.ds(i * cols, cols)], lsem.at[i]
        )
        copy.start()
        locals_.append(copy)
    pl.semaphore_wait(barrier, 8)

    halo = []
    for h in range(heads):
        hs = pl.ds(h * HD, HD)
        copies = []
        for slot, step in ((0, 1), (1, -1)):
            copies.append(send(k_ref.at[:, hs], kv.at[slot, 0, h], to_view[step]))
            copies.append(send(v_ref.at[:, hs], kv.at[slot, 1, h], to_view[step]))
        halo.append(copies)
    for copy in locals_:
        copy.wait()
    mine = wg.at[x, yl, yh, c]
    w_y1 = [send(mine, mine, to_y[s]) for s in (1, -1)]

    def transpose_chunk(i, _):
        chunk = normed[:, pl.ds(pl.multiple_of(i * 4 * rows, 128), 4 * rows)]
        turned = chunk.T.reshape(2, 2, rows, length)
        nt[lax.rem(i, 4), lax.div(i, 4)] = turned
        return 0

    lax.fori_loop(0, 8, transpose_chunk, 0)

    for copy in w_y1:
        copy.wait_recv()
    lo, hi = pl.ds(0, half), pl.ds(half, half)

    def block_y(yy):
        return lax.rem(yy, 2), lax.div(yy, 2)

    a0, a1 = block_y(y_dn)
    b0, b1 = block_y(y_up)
    from_dn = wg.at[x, a0, a1, c, lo]
    from_up = wg.at[x, b0, b1, c, hi]
    w_y2 = [send(from_dn, from_dn, to_y[1]), send(from_up, from_up, to_y[-1])]
    turned_copy = send(nt.at[:, :, :, 1 - c], ntp, partner)

    pen = [
        jnp.where(links[0, 0] >= 0, 0.0, -1e30).astype(F32),
        None,
        jnp.where(links[0, 1] >= 0, 0.0, -1e30).astype(F32),
    ]
    grad_halo = []
    w_x1, w_x2, w_par = [], [], []

    def attention(h):
        hs = slice(h * HD, (h + 1) * HD)
        for copy in halo[h]:
            copy.wait_recv()
        qh, gh = q_ref[:, hs], g_ref[:, hs]
        ks = [kv[0, 0, h], k_ref[:, hs], kv[1, 0, h]]
        vs = [kv[0, 1, h], v_ref[:, hs], kv[1, 1, h]]
        scores = []
        for j in range(3):
            s = dot(qh, ks[j], NT) * scaling
            scores.append(s if pen[j] is None else s + pen[j])
        top = jnp.maximum(jnp.maximum(scores[0], scores[1]), scores[2])
        top = jnp.max(top, axis=-1, keepdims=True)
        powers = [jnp.exp(s - top) for s in scores]
        total = jnp.sum(powers[0] + powers[1] + powers[2], axis=-1, keepdims=True)
        inv = 1.0 / total
        probs = [e * inv for e in powers]
        pgrads = [dot(gh, vj, NT) for vj in vs]
        delta = probs[0] * pgrads[0] + probs[1] * pgrads[1] + probs[2] * pgrads[2]
        delta = jnp.sum(delta, axis=-1, keepdims=True)
        sg = [(scaling * p * (d - delta)).astype(BF16) for p, d in zip(probs, pgrads)]
        query = dot(sg[0], ks[0], NN) + dot(sg[1], ks[1], NN) + dot(sg[2], ks[2], NN)
        hown[:, hs] = query.astype(BF16)
        for j, slot in ((0, 0), (2, 1)):
            gs[slot, h, 0] = dot(sg[j], qh, TN).astype(BF16)
            gs[slot, h, 1] = dot(probs[j].astype(BF16), gh, TN).astype(BF16)
        own[h, 0] = dot(sg[1], qh, TN)
        own[h, 1] = dot(probs[1].astype(BF16), gh, TN)
        grad_halo.append(
            [
                send(gs.at[0, h], gr.at[0, h], to_view[-1]),
                send(gs.at[1, h], gr.at[1, h], to_view[1]),
            ]
        )

    attention(0)
    for copy in w_y2:
        copy.wait_recv()
    column = wg.at[x, :, :, c]
    w_x1 = [send(column, column, to_x[s]) for s in (1, -1)]
    w_par.append(send(column, column, partner))
    for h in range(1, heads):
        attention(h)
        if h == 1:
            for copy in w_x1:
                copy.wait_recv()
            up, dn = wg.at[x_dn, 0, :, c], wg.at[x_up, 1, :, c]
            w_x2 = [send(up, up, to_x[1]), send(dn, dn, to_x[-1])]
            for xx in (x_dn, x_up):
                column = wg.at[xx, :, :, c]
                w_par.append(send(column, column, partner))
    hq = hown.at[:, pl.ds(0, cols)]
    q_copy = send(hq, hpar.at[:, pl.ds(0, cols)], partner)
    for copy in w_x2:
        copy.wait_recv()
    column = wg.at[x_far, :, :, c]
    w_par.append(send(column, column, partner))

    def weight_part(ci, x_first):
        cs = slice(ci * cols, (ci + 1) * cols)

        def step(xx, _):
            for ll in range(2):
                a = jnp.concatenate([nt[xx, ll, 0, c], nt[xx, ll, 1, c]], axis=0)
                b = ntp[xx, ll].reshape(2 * rows, length)
                acc = dot(a, hown[:, cs], NN) + dot(b, hpar[:, cs], NN)
                acc = acc.astype(BF16)
                for hh in range(2):
                    yy = hh * 2 + ll
                    block = acc[hh * rows : (hh + 1) * rows]
                    if x_first:
                        part[ci, xx, yy] = block
                    else:
                        part[ci, yy, xx] = block
            return 0

        lax.fori_loop(0, 4, step, 0)

    class Scatter:
        def __init__(self, ci, pa, to_a, pb, to_b):
            self.ci, self.pa, self.to_a, self.pb, self.to_b = ci, pa, to_a, pb, to_b
            self.aup, self.adn, self.afar = m(pa + 1, 4), m(pa - 1, 4), m(pa + 2, 4)
            self.bup, self.bdn, self.bfar = m(pb + 1, 4), m(pb - 1, 4), m(pb + 2, 4)

        def first(self):
            ci = self.ci
            low, high = pl.ds(0, 2), pl.ds(2, 2)
            self.f1 = [
                send(part.at[ci, self.afar, low], ra1.at[ci, 0], self.to_a[1]),
                send(part.at[ci, self.afar, high], ra1.at[ci, 1], self.to_a[-1]),
            ]
            self.f2 = [
                send(part.at[ci, self.aup, high], rra.at[ci, 0, high], self.to_a[1]),
                send(part.at[ci, self.adn, low], rra.at[ci, 1, low], self.to_a[-1]),
            ]

        def second(self):
            ci = self.ci
            low, high = pl.ds(0, 2), pl.ds(2, 2)
            for i, (block, piece, device) in enumerate(
                ((self.aup, low, self.to_a[1]), (self.adn, high, self.to_a[-1]))
            ):
                self.f1[i].wait_recv()
                old = part[ci, block, piece].astype(F32)
                part[ci, block, piece] = (old + ra1[ci, i].astype(F32)).astype(BF16)
                self.f2.append(send(part.at[ci, block, piece], rra.at[ci, i, piece], device))

        def third(self):
            ci = self.ci
            for copy in self.f2:
                copy.wait_recv()
            for j in range(4):
                value = part[ci, self.pa, j].astype(F32) + rra[ci, 0, j].astype(F32)
                rb[ci, j] = (value + rra[ci, 1, j].astype(F32)).astype(BF16)
            self.g1 = [
                send(rb.at[ci, self.bfar, lo], rb1.at[ci, 0], self.to_b[1]),
                send(rb.at[ci, self.bfar, hi], rb1.at[ci, 1], self.to_b[-1]),
            ]
            self.g2 = [
                send(rb.at[ci, self.bup, hi], rrb.at[ci, 0, hi], self.to_b[1]),
                send(rb.at[ci, self.bdn, lo], rrb.at[ci, 1, lo], self.to_b[-1]),
            ]

        def fourth(self):
            ci = self.ci
            for i, (block, piece, device) in enumerate(
                ((self.bup, lo, self.to_b[1]), (self.bdn, hi, self.to_b[-1]))
            ):
                self.g1[i].wait_recv()
                old = rb[ci, block, piece].astype(F32)
                rb[ci, block, piece] = (old + rb1[ci, i].astype(F32)).astype(BF16)
                self.g2.append(send(rb.at[ci, block, piece], rrb.at[ci, i, piece], device))

        def finish(self, out):
            ci = self.ci
            for copy in self.g2:
                copy.wait_recv()
            value = rb[ci, self.pb].astype(F32) + rrb[ci, 0].astype(F32)
            out[...] = (value + rrb[ci, 1].astype(F32)) * (1.0 / 32.0)

    rs_q = Scatter(0, x, to_x, y, to_y)
    rs_k = Scatter(1, x, to_x, y, to_y)
    rs_v = Scatter(2, y, to_y, x, to_x)

    turned_copy.wait_recv()
    q_copy.wait_recv()
    weight_part(0, True)
    rs_q.first()

    for h in range(heads):
        for copy in grad_halo[h]:
            copy.wait_recv()
        for i in range(2):
            value = own[h, i] + gr[0, h, i].astype(F32) + gr[1, h, i].astype(F32)
            start = (1 + i) * cols + h * HD
            hown[:, start : start + HD] = value.astype(BF16)
    hkv = pl.ds(cols, 2 * cols)
    kv_copy = send(hown.at[:, hkv], hpar.at[:, hkv], partner)
    rs_q.second()
    for copy in w_par:
        copy.wait_recv()

    def input_block(j):
        w = wg[lax.rem(j, 4), lax.div(j, 4)].reshape(4 * rows, 3 * cols)
        return dot(hown[...], w, NT)

    top_half, low_half = pl.ds(0, length // 2), pl.ds(length // 2, length // 2)
    far = m(z + 4, nz)
    zb[far] = input_block(far).astype(BF16)
    zs = [[
        send(zb.at[far, top_half], zr.at[0, 0, top_half], to_z[1]),
        send(zb.at[far, low_half], zr.at[1, 0, low_half], to_z[-1]),
    ]]
    for step in (3, 2):
        for sign in (1, -1):
            j = m(z + sign * step, nz)
            zb[j] = input_block(j).astype(BF16)

    def z_step(step):
        pieces = ((top_half, low_half) if step == 3 else (pl.ds(0, length),) * 2)
        new = []
        for i, sign in ((0, 1), (1, -1)):
            j = m(z + sign * step, nz)
            zs[-1][i].wait_recv()
            piece = pieces[i]
            value = zb[j, piece].astype(F32) + zr[i, 3 - step, piece].astype(F32)
            zb[j, piece] = value.astype(BF16)
            new.append(send(zb.at[j], zr.at[i, 4 - step], to_z[sign]))
        zs.append(new)

    z_step(3)
    kv_copy.wait_recv()
    weight_part(1, True)
    rs_k.first()
    weight_part(2, False)
    rs_v.first()
    z_step(2)
    rs_q.third()
    for sign in (1, -1):
        j = m(z + sign, nz)
        zb[j] = input_block(j).astype(BF16)
    rs_k.second()
    rs_v.second()
    z_step(1)
    rs_q.fourth()
    rs_v.third()
    rs_k.third()
    last = input_block(z)
    rs_q.finish(dq_out)
    rs_v.fourth()
    rs_k.fourth()
    for copy in zs[-1]:
        copy.wait_recv()
    dx_out[...] = (last + zr[0, 3].astype(F32) + zr[1, 3].astype(F32)).astype(BF16)
    rs_v.finish(dv_out)
    rs_k.finish(dk_out)
    for copy in started:
        copy.wait_send()


def body(normed, queries, keys, values, grads, links, wq, wk, wv):
    length, cols = queries.shape[2:]
    width = normed.shape[-1]
    heads = cols // HD
    rows = wq.shape[0]
    vmem = pl.BlockSpec(memory_space=pltpu.VMEM)
    count = 96
    out = pl.pallas_call(
        kernel,
        out_shape=(
            jax.ShapeDtypeStruct((length, cols), BF16),
            jax.ShapeDtypeStruct((rows, cols), F32),
            jax.ShapeDtypeStruct((rows, cols), F32),
            jax.ShapeDtypeStruct((rows, cols), F32),
        ),
        in_specs=[pl.BlockSpec(memory_space=pltpu.SMEM)] + [vmem] * 8,
        out_specs=(vmem,) * 4,
        scratch_shapes=[
            pltpu.VMEM((2, 2, heads, length, HD), BF16),
            pltpu.VMEM((4, 2, 2, 2, rows, 3 * cols), BF16),
            pltpu.VMEM((4, 2, 2, 2, rows, length), BF16),
            pltpu.VMEM((4, 2, 2, rows, length), BF16),
            pltpu.VMEM((length, 3 * cols), BF16),
            pltpu.VMEM((length, 3 * cols), BF16),
            pltpu.VMEM((heads, 2, length, HD), F32),
            pltpu.VMEM((2, heads, 2, length, HD), BF16),
            pltpu.VMEM((2, heads, 2, length, HD), BF16),
            pltpu.VMEM((3, 4, 4, rows, cols), BF16),
            pltpu.VMEM((3, 2, 2, rows, cols), BF16),
            pltpu.VMEM((3, 2, 4, rows, cols), BF16),
            pltpu.VMEM((3, 4, rows, cols), BF16),
            pltpu.VMEM((3, 2, rows // 2, cols), BF16),
            pltpu.VMEM((3, 2, rows, cols), BF16),
            pltpu.VMEM((8, length, cols), BF16),
            pltpu.VMEM((2, 4, length, cols), BF16),
            pltpu.SemaphoreType.DMA((count,)),
            pltpu.SemaphoreType.DMA((count,)),
            pltpu.SemaphoreType.DMA((3,)),
        ],
        compiler_params=pltpu.CompilerParams(
            collective_id=0, has_side_effects=True, vmem_limit_bytes=56 * 1024 * 1024
        ),
        name="attention_backward",
    )(
        links,
        normed.reshape(length, width),
        *(value.reshape(length, cols) for value in (queries, keys, values, grads)),
        wq, wk, wv,
    )
    return (out[0].reshape(1, 1, length, cols), out[1], out[2], out[3])


def solution(mesh):
    tokens = P("dp", "view", None, "head")
    weight = P(("dp", "view"), "head")
    return jax.shard_map(
        body,
        mesh=mesh,
        in_specs=(P("dp", "view", None, None),) + (tokens,) * 4 + (P("view", None),) + (weight,) * 3,
        out_specs=(tokens,) + (weight,) * 3,
        check_vma=False,
    )
```

```python
import contextlib

import jax
import jax.numpy as jnp
from jax import lax
from jax.experimental import pallas as pl
from jax.experimental.pallas import tpu as pltpu
from jax.sharding import PartitionSpec as P

HD = 128
SPLIT = 64
MESH = pl.DeviceIdType.MESH
F32 = jnp.float32
BF16 = jnp.bfloat16
NT = (((1,), (1,)), ((), ()))
NN = (((1,), (0,)), ((), ()))
TN = (((0,), (0,)), ((), ()))


def scope(name):
    return contextlib.nullcontext()


def dot(a, b, dims):
    return lax.dot_general(a, b, dims, preferred_element_type=F32)


def kernel(
    links, n_hbm, q_hbm, k_hbm, v_hbm, g_hbm, wq, wk, wv,
    dx_out, dq_out, dk_out, dv_out,
    normed, q_ref, k_ref, v_ref, g_ref,
    kv, wg, nt, ntp, hown, hpar, own, gs, gr, part, ra1, rra, rb, rb1, rrb, zb, zr,
    ssem, rsem, lsem,
):
    length, cols = q_ref.shape
    heads = cols // HD
    rows = wq.shape[0]
    half = rows // 2
    scaling = HD ** (-0.5)
    dp, vw, z = lax.axis_index("dp"), lax.axis_index("view"), lax.axis_index("head")
    nview, nz = 16, 8
    x = lax.div(vw, 4)
    yh = lax.rem(lax.div(vw, 2), 2)
    c = lax.rem(vw, 2)
    y = yh * 2 + dp

    def at(xx, yy, cc, zz):
        return (lax.rem(yy, 2), xx * 4 + lax.div(yy, 2) * 2 + cc, zz)

    def m(value, n):
        return lax.rem(value + n, n)

    x_up, x_dn, x_far = m(x + 1, 4), m(x - 1, 4), m(x + 2, 4)
    y_up, y_dn = m(y + 1, 4), m(y - 1, 4)
    to_x = {1: at(x_up, y, c, z), -1: at(x_dn, y, c, z)}
    to_y = {1: at(x, y_up, c, z), -1: at(x, y_dn, c, z)}
    to_z = {1: (dp, vw, m(z + 1, nz)), -1: (dp, vw, m(z - 1, nz))}
    to_view = {1: (dp, m(vw + 1, nview), z), -1: (dp, m(vw - 1, nview), z)}
    partner = at(x, y, 1 - c, z)

    started = []

    def send(src, dst, device):
        slot = len(started)
        copy = pltpu.make_async_remote_copy(
            src_ref=src, dst_ref=dst, send_sem=ssem.at[slot], recv_sem=rsem.at[slot],
            device_id=device, device_id_type=MESH,
        )
        copy.start()
        started.append(copy)
        return copy

    barrier = pltpu.get_barrier_semaphore()
    for peers in (to_view, to_x, to_y, to_z):
        for step in (1, -1):
            pl.semaphore_signal(barrier, inc=1, device_id=peers[step], device_id_type=MESH)
    yl = dp

    def load(src, dst, slot):
        copy = pltpu.make_async_copy(src, dst, lsem.at[slot])
        copy.start()
        return copy

    w_loads = [
        load(w, wg.at[x, yl, yh, c, :, pl.ds(i * cols, cols)], i)
        for i, w in enumerate((wq, wk, wv))
    ]
    kv_loads = [load(k_hbm, k_ref, 3), load(v_hbm, v_ref, 4)]
    loads = [load(q_hbm, q_ref, 5), load(g_hbm, g_ref, 6), load(n_hbm, normed, 7)]
    for copy in w_loads + kv_loads:
        copy.wait()
    with scope("barrier"):
        pl.semaphore_wait(barrier, 8)

    class Gather:
        def __init__(self, start, size, x_first):
            self.x_first = x_first
            self.all = pl.ds(start, size)
            self.lo, self.hi = pl.ds(start, size // 2), pl.ds(start + size // 2, size // 2)
            self.to_a, self.to_b = (to_x, to_y) if x_first else (to_y, to_x)
            self.b1, self.b2, self.par = {}, {}, []

        def ref(self, ao, bo, piece):
            xo, yo = (ao, bo) if self.x_first else (bo, ao)
            yy = m(y + yo, 4)
            return wg.at[m(x + xo, 4), lax.rem(yy, 2), lax.div(yy, 2), c, piece]

        def pass_on(self, ao, bo, piece, device):
            block = self.ref(ao, bo, piece)
            return send(block, block, device)

        def start(self):
            self.a1 = [self.pass_on(0, 0, self.all, self.to_a[s]) for s in (1, -1)]

        def across(self, ao):
            self.b1[ao] = [self.pass_on(ao, 0, self.all, self.to_b[s]) for s in (1, -1)]

        def forward(self):
            for copy in self.a1:
                copy.wait_recv()
            self.a2 = [
                self.pass_on(-1, 0, self.lo, self.to_a[1]),
                self.pass_on(1, 0, self.hi, self.to_a[-1]),
            ]

        def far(self):
            for copy in self.a2:
                copy.wait_recv()

        def across_forward(self, ao):
            for copy in self.b1[ao]:
                copy.wait_recv()
            self.b2[ao] = [
                self.pass_on(ao, -1, self.lo, self.to_b[1]),
                self.pass_on(ao, 1, self.hi, self.to_b[-1]),
            ]

        def across_far(self):
            for copies in self.b2.values():
                for copy in copies:
                    copy.wait_recv()

        def to_partner(self, bo):
            if self.x_first:
                yy = m(y + bo, 4)
                block = wg.at[:, lax.rem(yy, 2), lax.div(yy, 2), c, self.all]
            else:
                block = wg.at[m(x + bo, 4), :, :, c, self.all]
            self.par.append(send(block, block, partner))

    ga = Gather(0, SPLIT, False)
    gb = Gather(SPLIT, rows - SPLIT, True)
    ga.start()
    gb.start()
    ga.across(0)
    halo = []
    for h in range(heads):
        hs = pl.ds(h * HD, HD)
        copies = []
        for slot, step in ((0, 1), (1, -1)):
            copies.append(send(k_ref.at[:, hs], kv.at[slot, 0, h], to_view[step]))
            copies.append(send(v_ref.at[:, hs], kv.at[slot, 1, h], to_view[step]))
        halo.append(copies)
    gb.across(0)
    for copy in loads:
        copy.wait()
    lo, hi = pl.ds(0, half), pl.ds(half, half)

    def transpose_chunk(i, _):
        chunk = normed[:, pl.ds(pl.multiple_of(i * 4 * rows, 128), 4 * rows)]
        turned = chunk.T.reshape(2, 2, rows, length)
        nt[lax.rem(i, 4), lax.div(i, 4)] = turned
        return 0

    with scope("transpose"):
        lax.fori_loop(0, 8, transpose_chunk, 0)
    with scope("ga_forward"):
        ga.forward()
        ga.across(-1)
        ga.across(1)
    with scope("gb_forward"):
        gb.forward()
    turned_copy = send(nt.at[:, :, :, 1 - c], ntp, partner)
    with scope("ga_af0"):
        ga.across_forward(0)
    with scope("ga_far"):
        ga.far()
        ga.across(2)
        ga.to_partner(0)

    pen = [
        jnp.where(links[0, 0] >= 0, 0.0, -1e30).astype(F32),
        None,
        jnp.where(links[0, 1] >= 0, 0.0, -1e30).astype(F32),
    ]
    grad_halo = []
    w_x1, w_x2, w_par = [], [], []

    def attention(h):
        hs = slice(h * HD, (h + 1) * HD)
        for copy in halo[h]:
            copy.wait_recv()
        qh, gh = q_ref[:, hs], g_ref[:, hs]
        ks = [kv[0, 0, h], k_ref[:, hs], kv[1, 0, h]]
        vs = [kv[0, 1, h], v_ref[:, hs], kv[1, 1, h]]
        scores = []
        for j in range(3):
            s = dot(qh, ks[j], NT) * scaling
            scores.append(s if pen[j] is None else s + pen[j])
        top = jnp.maximum(jnp.maximum(scores[0], scores[1]), scores[2])
        top = jnp.max(top, axis=-1, keepdims=True)
        powers = [jnp.exp(s - top) for s in scores]
        total = jnp.sum(powers[0] + powers[1] + powers[2], axis=-1, keepdims=True)
        inv = 1.0 / total
        probs = [e * inv for e in powers]
        pgrads = [dot(gh, vj, NT) for vj in vs]
        delta = probs[0] * pgrads[0] + probs[1] * pgrads[1] + probs[2] * pgrads[2]
        delta = jnp.sum(delta, axis=-1, keepdims=True)
        sg = [(scaling * p * (d - delta)).astype(BF16) for p, d in zip(probs, pgrads)]
        query = dot(sg[0], ks[0], NN) + dot(sg[1], ks[1], NN) + dot(sg[2], ks[2], NN)
        hown[:, hs] = query.astype(BF16)
        for j, slot in ((0, 0), (2, 1)):
            gs[slot, h, 0] = dot(sg[j], qh, TN).astype(BF16)
            gs[slot, h, 1] = dot(probs[j].astype(BF16), gh, TN).astype(BF16)
        own[h, 0] = dot(sg[1], qh, TN)
        own[h, 1] = dot(probs[1].astype(BF16), gh, TN)
        grad_halo.append(
            [
                send(gs.at[0, h], gr.at[0, h], to_view[-1]),
                send(gs.at[1, h], gr.at[1, h], to_view[1]),
            ]
        )

    for h in range(heads):
        with scope("att"):
            attention(h)
    hq = hown.at[:, pl.ds(0, cols)]
    q_copy = send(hq, hpar.at[:, pl.ds(0, cols)], partner)
    with scope("gb_far"):
        gb.across(-1)
        gb.across(1)
        gb.far()
        gb.across(2)
        gb.to_partner(0)
    with scope("ga_af1"):
        ga.across_forward(-1)
        ga.across_forward(1)
    with scope("gb_af0"):
        gb.across_forward(0)
    with scope("ga_af2"):
        ga.across_forward(2)
        ga.to_partner(-1)
        ga.to_partner(1)

    def weight_part(ci, x_first):
        cs = slice(ci * cols, (ci + 1) * cols)

        def step(xx, _):
            for ll in range(2):
                a = jnp.concatenate([nt[xx, ll, 0, c], nt[xx, ll, 1, c]], axis=0)
                b = ntp[xx, ll].reshape(2 * rows, length)
                acc = dot(a, hown[:, cs], NN) + dot(b, hpar[:, cs], NN)
                acc = acc.astype(BF16)
                for hh in range(2):
                    yy = hh * 2 + ll
                    block = acc[hh * rows : (hh + 1) * rows]
                    if x_first:
                        part[ci, xx, yy] = block
                    else:
                        part[ci, yy, xx] = block
            return 0

        lax.fori_loop(0, 4, step, 0)

    class Scatter:
        def __init__(self, ci, pa, to_a, pb, to_b):
            self.ci, self.pa, self.to_a, self.pb, self.to_b = ci, pa, to_a, pb, to_b
            self.aup, self.adn, self.afar = m(pa + 1, 4), m(pa - 1, 4), m(pa + 2, 4)
            self.bup, self.bdn, self.bfar = m(pb + 1, 4), m(pb - 1, 4), m(pb + 2, 4)

        def first(self):
            ci = self.ci
            low, high = pl.ds(0, 2), pl.ds(2, 2)
            self.f1 = [
                send(part.at[ci, self.afar, low], ra1.at[ci, 0], self.to_a[1]),
                send(part.at[ci, self.afar, high], ra1.at[ci, 1], self.to_a[-1]),
            ]
            self.f2 = [
                send(part.at[ci, self.aup, high], rra.at[ci, 0, high], self.to_a[1]),
                send(part.at[ci, self.adn, low], rra.at[ci, 1, low], self.to_a[-1]),
            ]

        def second(self):
            ci = self.ci
            low, high = pl.ds(0, 2), pl.ds(2, 2)
            for i, (block, piece, device) in enumerate(
                ((self.aup, low, self.to_a[1]), (self.adn, high, self.to_a[-1]))
            ):
                self.f1[i].wait_recv()
                old = part[ci, block, piece].astype(F32)
                part[ci, block, piece] = (old + ra1[ci, i].astype(F32)).astype(BF16)
                self.f2.append(send(part.at[ci, block, piece], rra.at[ci, i, piece], device))

        def third(self):
            ci = self.ci
            for copy in self.f2:
                copy.wait_recv()
            for j in range(4):
                value = part[ci, self.pa, j].astype(F32) + rra[ci, 0, j].astype(F32)
                rb[ci, j] = (value + rra[ci, 1, j].astype(F32)).astype(BF16)
            self.g1 = [
                send(rb.at[ci, self.bfar, lo], rb1.at[ci, 0], self.to_b[1]),
                send(rb.at[ci, self.bfar, hi], rb1.at[ci, 1], self.to_b[-1]),
            ]
            self.g2 = [
                send(rb.at[ci, self.bup, hi], rrb.at[ci, 0, hi], self.to_b[1]),
                send(rb.at[ci, self.bdn, lo], rrb.at[ci, 1, lo], self.to_b[-1]),
            ]

        def fourth(self):
            ci = self.ci
            for i, (block, piece, device) in enumerate(
                ((self.bup, lo, self.to_b[1]), (self.bdn, hi, self.to_b[-1]))
            ):
                self.g1[i].wait_recv()
                old = rb[ci, block, piece].astype(F32)
                rb[ci, block, piece] = (old + rb1[ci, i].astype(F32)).astype(BF16)
                self.g2.append(send(rb.at[ci, block, piece], rrb.at[ci, i, piece], device))

        def finish(self, out):
            ci = self.ci
            for copy in self.g2:
                copy.wait_recv()
            value = rb[ci, self.pb].astype(F32) + rrb[ci, 0].astype(F32)
            out[...] = (value + rrb[ci, 1].astype(F32)) * (1.0 / 32.0)

    rs_q = Scatter(0, y, to_y, x, to_x)
    rs_k = Scatter(1, x, to_x, y, to_y)
    rs_v = Scatter(2, y, to_y, x, to_x)

    with scope("wp_q"):
        turned_copy.wait_recv()
        q_copy.wait_recv()
        weight_part(0, False)
    with scope("gb_af1"):
        gb.across_forward(-1)
        gb.across_forward(1)
    with scope("gb_af2"):
        gb.across_forward(2)
        gb.to_partner(-1)
        gb.to_partner(1)
    rs_q.first()
    with scope("gh_wait"):
        for h in range(heads):
            for copy in grad_halo[h]:
                copy.wait_recv()
            for i in range(2):
                value = own[h, i] + gr[0, h, i].astype(F32) + gr[1, h, i].astype(F32)
                start = (1 + i) * cols + h * HD
                hown[:, start : start + HD] = value.astype(BF16)
    hkv = pl.ds(cols, 2 * cols)
    kv_copy = send(hown.at[:, hkv], hpar.at[:, hkv], partner)
    with scope("ga_bf"):
        ga.across_far()
        ga.to_partner(2)
    with scope("gb_bf"):
        gb.across_far()
        gb.to_partner(2)
    with scope("wpar"):
        for copy in ga.par + gb.par:
            copy.wait_recv()

    def input_block(j):
        w = wg[lax.rem(j, 4), lax.div(j, 4)].reshape(4 * rows, 3 * cols)
        return dot(hown[...], w, NT)

    part_rows = length // 2
    half_rows = part_rows // 2
    far = m(z + 4, nz)
    with scope("zfar"):
        zb[far] = input_block(far).astype(BF16)
    zs = [[], []]
    for p in range(2):
        for i, sign in ((0, 1), (1, -1)):
            piece = pl.ds(p * part_rows + i * half_rows, half_rows)
            zs[p].append(send(zb.at[far, piece], zr.at[i, 0, piece], to_z[sign]))

    def z_block(step):
        with scope("zb"):
            for sign in (1, -1):
                j = m(z + sign * step, nz)
                zb[j] = input_block(j).astype(BF16)

    def z_step(step, p):
        with scope("z%d%d" % (step, p)):
            new = []
            whole = pl.ds(p * part_rows, part_rows)
            for i, sign in ((0, 1), (1, -1)):
                piece = pl.ds(p * part_rows + i * half_rows, half_rows) if step == 3 else whole
                j = m(z + sign * step, nz)
                zs[p][i].wait_recv()
                value = zb[j, piece].astype(F32) + zr[i, 3 - step, piece].astype(F32)
                zb[j, piece] = value.astype(BF16)
                new.append(send(zb.at[j, whole], zr.at[i, 4 - step, whole], to_z[sign]))
            zs[p] = new

    z_block(3)
    z_block(2)
    with scope("wp_k"):
        kv_copy.wait_recv()
        weight_part(1, True)
    rs_k.first()
    z_step(3, 0)
    z_step(3, 1)
    with scope("wp_v"):
        weight_part(2, False)
    rs_v.first()
    with scope("q2"):
        rs_q.second()
    z_step(2, 0)
    z_step(2, 1)
    z_block(1)
    with scope("k2"):
        rs_k.second()
    with scope("q3"):
        rs_q.third()
    with scope("v2"):
        rs_v.second()
    z_step(1, 0)
    z_step(1, 1)
    with scope("k3"):
        rs_k.third()
    with scope("q4"):
        rs_q.fourth()
    with scope("v3"):
        rs_v.third()
    last = input_block(z)
    with scope("k4"):
        rs_k.fourth()
    with scope("v4"):
        rs_v.fourth()
    with scope("q5"):
        rs_q.finish(dq_out)
    with scope("zlast"):
        for copies in zs:
            for copy in copies:
                copy.wait_recv()
        dx_out[...] = (last + zr[0, 3].astype(F32) + zr[1, 3].astype(F32)).astype(BF16)
    with scope("k5"):
        rs_k.finish(dk_out)
    with scope("v5"):
        rs_v.finish(dv_out)
    for copy in started:
        copy.wait_send()


def publish(a, b, c, d, oa, ob, oc, od):
    for src, dst in ((a, oa), (b, ob), (c, oc), (d, od)):
        dst[...] = src[...]


def body(normed, queries, keys, values, grads, links, wq, wk, wv):
    length, cols = queries.shape[2:]
    width = normed.shape[-1]
    heads = cols // HD
    rows = wq.shape[0]
    vmem = pl.BlockSpec(memory_space=pltpu.VMEM)
    anywhere = pl.BlockSpec(memory_space=pl.ANY)
    count = 144
    out = pl.pallas_call(
        kernel,
        out_shape=(
            jax.ShapeDtypeStruct((length, cols), BF16),
            jax.ShapeDtypeStruct((rows, cols), F32),
            jax.ShapeDtypeStruct((rows, cols), F32),
            jax.ShapeDtypeStruct((rows, cols), F32),
        ),
        in_specs=[pl.BlockSpec(memory_space=pltpu.SMEM)] + [anywhere] * 8,
        out_specs=(vmem,) * 4,
        scratch_shapes=[
            pltpu.VMEM((length, width), BF16),
            *[pltpu.VMEM((length, cols), BF16)] * 4,
            pltpu.VMEM((2, 2, heads, length, HD), BF16),
            pltpu.VMEM((4, 2, 2, 2, rows, 3 * cols), BF16),
            pltpu.VMEM((4, 2, 2, 2, rows, length), BF16),
            pltpu.VMEM((4, 2, 2, rows, length), BF16),
            pltpu.VMEM((length, 3 * cols), BF16),
            pltpu.VMEM((length, 3 * cols), BF16),
            pltpu.VMEM((heads, 2, length, HD), F32),
            pltpu.VMEM((2, heads, 2, length, HD), BF16),
            pltpu.VMEM((2, heads, 2, length, HD), BF16),
            pltpu.VMEM((3, 4, 4, rows, cols), BF16),
            pltpu.VMEM((3, 2, 2, rows, cols), BF16),
            pltpu.VMEM((3, 2, 4, rows, cols), BF16),
            pltpu.VMEM((3, 4, rows, cols), BF16),
            pltpu.VMEM((3, 2, rows // 2, cols), BF16),
            pltpu.VMEM((3, 2, rows, cols), BF16),
            pltpu.VMEM((8, length, cols), BF16),
            pltpu.VMEM((2, 4, length, cols), BF16),
            pltpu.SemaphoreType.DMA((count,)),
            pltpu.SemaphoreType.DMA((count,)),
            pltpu.SemaphoreType.DMA((8,)),
        ],
        compiler_params=pltpu.CompilerParams(
            collective_id=0, has_side_effects=True, vmem_limit_bytes=56 * 1024 * 1024
        ),
        name="attention_backward",
    )(
        links,
        normed.reshape(length, width),
        *(value.reshape(length, cols) for value in (queries, keys, values, grads)),
        wq, wk, wv,
    )
    out = pl.pallas_call(
        publish,
        out_shape=[jax.ShapeDtypeStruct(o.shape, o.dtype) for o in out],
        in_specs=[vmem] * 4,
        out_specs=[vmem] * 4,
        name="publish",
    )(*out)
    return (out[0].reshape(1, 1, length, cols), out[1], out[2], out[3])


def solution(mesh):
    tokens = P("dp", "view", None, "head")
    weight = P(("dp", "view"), "head")
    return jax.shard_map(
        body,
        mesh=mesh,
        in_specs=(P("dp", "view", None, None),) + (tokens,) * 4 + (P("view", None),) + (weight,) * 3,
        out_specs=(tokens,) + (weight,) * 3,
        check_vma=False,
    )
```

```python
import contextlib

import jax
import jax.numpy as jnp
from jax import lax
from jax.experimental import pallas as pl
from jax.experimental.pallas import tpu as pltpu
from jax.sharding import PartitionSpec as P

HD = 128
MESH = pl.DeviceIdType.MESH
F32 = jnp.float32
BF16 = jnp.bfloat16
NT = (((1,), (1,)), ((), ()))
NN = (((1,), (0,)), ((), ()))
TN = (((0,), (0,)), ((), ()))


def scope(name):
    return contextlib.nullcontext()


def dot(a, b, dims):
    return lax.dot_general(a, b, dims, preferred_element_type=F32)


def kernel(
    links, n_hbm, q_hbm, k_hbm, v_hbm, g_hbm, wq, wk, wv,
    dx_out, dq_out, dk_out, dv_out,
    normed, q_ref, k_ref, v_ref, g_ref,
    kv, wg, nt, ntp, hown, hpar, own, gs, gr, part, ra1, rra, rb, rb1, rrb, zb, zr,
    ssem, rsem, lsem,
):
    length, cols = q_ref.shape
    heads = cols // HD
    rows = wq.shape[0]
    half = rows // 2
    scaling = HD ** (-0.5)
    dp, vw, z = lax.axis_index("dp"), lax.axis_index("view"), lax.axis_index("head")
    nview, nz = 16, 8
    x = lax.div(vw, 4)
    yh = lax.rem(lax.div(vw, 2), 2)
    c = lax.rem(vw, 2)
    y = yh * 2 + dp

    def at(xx, yy, cc, zz):
        return (lax.rem(yy, 2), xx * 4 + lax.div(yy, 2) * 2 + cc, zz)

    def m(value, n):
        return lax.rem(value + n, n)

    x_up, x_dn, x_far = m(x + 1, 4), m(x - 1, 4), m(x + 2, 4)
    y_up, y_dn = m(y + 1, 4), m(y - 1, 4)
    to_x = {1: at(x_up, y, c, z), -1: at(x_dn, y, c, z)}
    to_y = {1: at(x, y_up, c, z), -1: at(x, y_dn, c, z)}
    to_z = {1: (dp, vw, m(z + 1, nz)), -1: (dp, vw, m(z - 1, nz))}
    to_view = {1: (dp, m(vw + 1, nview), z), -1: (dp, m(vw - 1, nview), z)}
    partner = at(x, y, 1 - c, z)

    started = []

    def send(src, dst, device):
        slot = len(started)
        copy = pltpu.make_async_remote_copy(
            src_ref=src, dst_ref=dst, send_sem=ssem.at[slot], recv_sem=rsem.at[slot],
            device_id=device, device_id_type=MESH,
        )
        copy.start()
        started.append(copy)
        return copy

    barrier = pltpu.get_barrier_semaphore()
    for peers in (to_view, to_x, to_y, to_z):
        for step in (1, -1):
            pl.semaphore_signal(barrier, inc=1, device_id=peers[step], device_id_type=MESH)
    yl = dp

    def load(src, dst, slot):
        copy = pltpu.make_async_copy(src, dst, lsem.at[slot])
        copy.start()
        return copy

    w_loads = [
        load(w, wg.at[x, yl, yh, c, :, pl.ds(i * cols, cols)], i)
        for i, w in enumerate((wq, wk, wv))
    ]
    kv_loads = [load(k_hbm, k_ref, 3), load(v_hbm, v_ref, 4)]
    loads = [load(q_hbm, q_ref, 5), load(g_hbm, g_ref, 6), load(n_hbm, normed, 7)]
    for copy in w_loads + kv_loads:
        copy.wait()
    with scope("barrier"):
        pl.semaphore_wait(barrier, 8)

    class Gather:
        def __init__(self, start, size, x_first):
            self.x_first = x_first
            self.all = pl.ds(start, size)
            self.lo, self.hi = pl.ds(start, size // 2), pl.ds(start + size // 2, size // 2)
            self.to_a, self.to_b = (to_x, to_y) if x_first else (to_y, to_x)
            self.b1, self.b2, self.par = {}, {}, []

        def ref(self, ao, bo, piece):
            xo, yo = (ao, bo) if self.x_first else (bo, ao)
            yy = m(y + yo, 4)
            return wg.at[m(x + xo, 4), lax.rem(yy, 2), lax.div(yy, 2), c, piece]

        def pass_on(self, ao, bo, piece, device):
            block = self.ref(ao, bo, piece)
            return send(block, block, device)

        def start(self):
            self.a1 = [self.pass_on(0, 0, self.all, self.to_a[s]) for s in (1, -1)]

        def across(self, ao):
            self.b1[ao] = [self.pass_on(ao, 0, self.all, self.to_b[s]) for s in (1, -1)]

        def forward(self):
            for copy in self.a1:
                copy.wait_recv()
            self.a2 = [
                self.pass_on(-1, 0, self.lo, self.to_a[1]),
                self.pass_on(1, 0, self.hi, self.to_a[-1]),
            ]

        def far(self):
            for copy in self.a2:
                copy.wait_recv()

        def across_forward(self, ao):
            for copy in self.b1[ao]:
                copy.wait_recv()
            third = rows // 3
            turn = 1 - 2 * yh
            turn_to = at(m(x + turn, 4), y, c, z)
            self.b2[ao] = [
                self.pass_on(ao, -1, pl.ds(0, third), to_x[1]),
                self.pass_on(ao, 1, pl.ds(2 * third, third), to_x[-1]),
                self.pass_on(ao, -turn, pl.ds(third, third), turn_to),
            ]

        def across_far(self, ao):
            for copy in self.b2[ao]:
                copy.wait_recv()
            self.par.append(self.pass_on(ao, 2, self.all, partner))

        def to_partner(self, bo):
            if self.x_first:
                yy = m(y + bo, 4)
                block = wg.at[:, lax.rem(yy, 2), lax.div(yy, 2), c, self.all]
            else:
                block = wg.at[m(x + bo, 4), :, :, c, self.all]
            self.par.append(send(block, block, partner))

    gather = Gather(0, rows, False)
    gather.start()
    gather.across(0)
    halo = []
    for h in range(heads):
        hs = pl.ds(h * HD, HD)
        copies = []
        for slot, step in ((0, 1), (1, -1)):
            copies.append(send(k_ref.at[:, hs], kv.at[slot, 0, h], to_view[step]))
            copies.append(send(v_ref.at[:, hs], kv.at[slot, 1, h], to_view[step]))
        halo.append(copies)
    for copy in loads:
        copy.wait()
    lo, hi = pl.ds(0, half), pl.ds(half, half)

    def transpose_chunk(i, _):
        chunk = normed[:, pl.ds(pl.multiple_of(i * 4 * rows, 128), 4 * rows)]
        turned = chunk.T.reshape(2, 2, rows, length)
        nt[lax.rem(i, 4), lax.div(i, 4)] = turned
        return 0

    with scope("transpose"):
        lax.fori_loop(0, 8, transpose_chunk, 0)
    with scope("ga_forward"):
        gather.forward()
        gather.across(-1)
        gather.across(1)
    turned_copy = send(nt.at[:, :, :, 1 - c], ntp, partner)
    with scope("ga_af0"):
        gather.across_forward(0)

    pen = [
        jnp.where(links[0, 0] >= 0, 0.0, -1e30).astype(F32),
        None,
        jnp.where(links[0, 1] >= 0, 0.0, -1e30).astype(F32),
    ]
    grad_halo = []
    w_x1, w_x2, w_par = [], [], []

    def attention(h):
        hs = slice(h * HD, (h + 1) * HD)
        for copy in halo[h]:
            copy.wait_recv()
        qh, gh = q_ref[:, hs], g_ref[:, hs]
        ks = [kv[0, 0, h], k_ref[:, hs], kv[1, 0, h]]
        vs = [kv[0, 1, h], v_ref[:, hs], kv[1, 1, h]]
        scores = []
        for j in range(3):
            s = dot(qh, ks[j], NT) * scaling
            scores.append(s if pen[j] is None else s + pen[j])
        top = jnp.maximum(jnp.maximum(scores[0], scores[1]), scores[2])
        top = jnp.max(top, axis=-1, keepdims=True)
        powers = [jnp.exp(s - top) for s in scores]
        total = jnp.sum(powers[0] + powers[1] + powers[2], axis=-1, keepdims=True)
        inv = 1.0 / total
        probs = [e * inv for e in powers]
        pgrads = [dot(gh, vj, NT) for vj in vs]
        delta = probs[0] * pgrads[0] + probs[1] * pgrads[1] + probs[2] * pgrads[2]
        delta = jnp.sum(delta, axis=-1, keepdims=True)
        sg = [(scaling * p * (d - delta)).astype(BF16) for p, d in zip(probs, pgrads)]
        query = dot(sg[0], ks[0], NN) + dot(sg[1], ks[1], NN) + dot(sg[2], ks[2], NN)
        hown[:, hs] = query.astype(BF16)
        for j, slot in ((0, 0), (2, 1)):
            gs[slot, h, 0] = dot(sg[j], qh, TN).astype(BF16)
            gs[slot, h, 1] = dot(probs[j].astype(BF16), gh, TN).astype(BF16)
        own[h, 0] = dot(sg[1], qh, TN)
        own[h, 1] = dot(probs[1].astype(BF16), gh, TN)
        grad_halo.append(
            [
                send(gs.at[0, h], gr.at[0, h], to_view[-1]),
                send(gs.at[1, h], gr.at[1, h], to_view[1]),
            ]
        )

    for h in range(heads):
        with scope("att"):
            attention(h)
    hq = hown.at[:, pl.ds(0, cols)]
    q_copy = send(hq, hpar.at[:, pl.ds(0, cols)], partner)
    with scope("ga_far"):
        gather.far()
        gather.across(2)
        gather.to_partner(0)
    with scope("ga_af1"):
        gather.across_forward(-1)
        gather.across_forward(1)

    def weight_part(ci, x_first):
        cs = slice(ci * cols, (ci + 1) * cols)

        def step(xx, _):
            for ll in range(2):
                a = jnp.concatenate([nt[xx, ll, 0, c], nt[xx, ll, 1, c]], axis=0)
                b = ntp[xx, ll].reshape(2 * rows, length)
                acc = dot(a, hown[:, cs], NN) + dot(b, hpar[:, cs], NN)
                acc = acc.astype(BF16)
                for hh in range(2):
                    yy = hh * 2 + ll
                    block = acc[hh * rows : (hh + 1) * rows]
                    if x_first:
                        part[ci, xx, yy] = block
                    else:
                        part[ci, yy, xx] = block
            return 0

        lax.fori_loop(0, 4, step, 0)

    class Scatter:
        def __init__(self, ci, pa, to_a, pb, to_b):
            self.ci, self.pa, self.to_a, self.pb, self.to_b = ci, pa, to_a, pb, to_b
            self.aup, self.adn, self.afar = m(pa + 1, 4), m(pa - 1, 4), m(pa + 2, 4)
            self.bup, self.bdn, self.bfar = m(pb + 1, 4), m(pb - 1, 4), m(pb + 2, 4)

        def first(self):
            ci = self.ci
            low, high = pl.ds(0, 2), pl.ds(2, 2)
            self.f1 = [
                send(part.at[ci, self.afar, low], ra1.at[ci, 0], self.to_a[1]),
                send(part.at[ci, self.afar, high], ra1.at[ci, 1], self.to_a[-1]),
            ]
            self.f2 = [
                send(part.at[ci, self.aup, high], rra.at[ci, 0, high], self.to_a[1]),
                send(part.at[ci, self.adn, low], rra.at[ci, 1, low], self.to_a[-1]),
            ]

        def second(self):
            ci = self.ci
            low, high = pl.ds(0, 2), pl.ds(2, 2)
            for i, (block, piece, device) in enumerate(
                ((self.aup, low, self.to_a[1]), (self.adn, high, self.to_a[-1]))
            ):
                self.f1[i].wait_recv()
                old = part[ci, block, piece].astype(F32)
                part[ci, block, piece] = (old + ra1[ci, i].astype(F32)).astype(BF16)
                self.f2.append(send(part.at[ci, block, piece], rra.at[ci, i, piece], device))

        def third(self):
            ci = self.ci
            for copy in self.f2:
                copy.wait_recv()
            for j in range(4):
                value = part[ci, self.pa, j].astype(F32) + rra[ci, 0, j].astype(F32)
                rb[ci, j] = (value + rra[ci, 1, j].astype(F32)).astype(BF16)
            self.g1 = [
                send(rb.at[ci, self.bfar, lo], rb1.at[ci, 0], self.to_b[1]),
                send(rb.at[ci, self.bfar, hi], rb1.at[ci, 1], self.to_b[-1]),
            ]
            self.g2 = [
                send(rb.at[ci, self.bup, hi], rrb.at[ci, 0, hi], self.to_b[1]),
                send(rb.at[ci, self.bdn, lo], rrb.at[ci, 1, lo], self.to_b[-1]),
            ]

        def fourth(self):
            ci = self.ci
            for i, (block, piece, device) in enumerate(
                ((self.bup, lo, self.to_b[1]), (self.bdn, hi, self.to_b[-1]))
            ):
                self.g1[i].wait_recv()
                old = rb[ci, block, piece].astype(F32)
                rb[ci, block, piece] = (old + rb1[ci, i].astype(F32)).astype(BF16)
                self.g2.append(send(rb.at[ci, block, piece], rrb.at[ci, i, piece], device))

        def finish(self, out):
            ci = self.ci
            for copy in self.g2:
                copy.wait_recv()
            value = rb[ci, self.pb].astype(F32) + rrb[ci, 0].astype(F32)
            out[...] = (value + rrb[ci, 1].astype(F32)) * (1.0 / 32.0)

    rs_q = Scatter(0, y, to_y, x, to_x)
    rs_k = Scatter(1, x, to_x, y, to_y)
    rs_v = Scatter(2, y, to_y, x, to_x)

    with scope("wp_q"):
        turned_copy.wait_recv()
        q_copy.wait_recv()
        weight_part(0, False)
    rs_q.first()
    with scope("gh_wait"):
        for h in range(heads):
            for copy in grad_halo[h]:
                copy.wait_recv()
            for i in range(2):
                value = own[h, i] + gr[0, h, i].astype(F32) + gr[1, h, i].astype(F32)
                start = (1 + i) * cols + h * HD
                hown[:, start : start + HD] = value.astype(BF16)
    hkv = pl.ds(cols, 2 * cols)
    kv_copy = send(hown.at[:, hkv], hpar.at[:, hkv], partner)
    with scope("ga_af2"):
        gather.across_forward(2)
        gather.to_partner(-1)
        gather.to_partner(1)
    with scope("q2"):
        rs_q.second()
    with scope("wp_v"):
        kv_copy.wait_recv()
        weight_part(2, False)
    rs_v.first()
    with scope("wp_k"):
        weight_part(1, True)
    rs_k.first()
    with scope("ga_bf"):
        for ao in (0, -1, 1, 2):
            gather.across_far(ao)
    with scope("wpar"):
        for copy in gather.par:
            copy.wait_recv()

    def input_block(j):
        w = wg[lax.rem(j, 4), lax.div(j, 4)].reshape(4 * rows, 3 * cols)
        return dot(hown[...], w, NT)

    part_rows = length // 2
    half_rows = part_rows // 2
    far = m(z + 4, nz)
    with scope("zfar"):
        zb[far] = input_block(far).astype(BF16)
    zs = [[], []]
    for p in range(2):
        for i, sign in ((0, 1), (1, -1)):
            piece = pl.ds(p * part_rows + i * half_rows, half_rows)
            zs[p].append(send(zb.at[far, piece], zr.at[i, 0, piece], to_z[sign]))

    def z_block(step):
        with scope("zb"):
            for sign in (1, -1):
                j = m(z + sign * step, nz)
                zb[j] = input_block(j).astype(BF16)

    def z_step(step, p):
        with scope("z%d%d" % (step, p)):
            new = []
            whole = pl.ds(p * part_rows, part_rows)
            for i, sign in ((0, 1), (1, -1)):
                piece = pl.ds(p * part_rows + i * half_rows, half_rows) if step == 3 else whole
                j = m(z + sign * step, nz)
                zs[p][i].wait_recv()
                value = zb[j, piece].astype(F32) + zr[i, 3 - step, piece].astype(F32)
                zb[j, piece] = value.astype(BF16)
                new.append(send(zb.at[j, whole], zr.at[i, 4 - step, whole], to_z[sign]))
            zs[p] = new

    z_block(3)
    with scope("q3"):
        rs_q.third()
    z_block(2)
    with scope("v2"):
        rs_v.second()
    z_step(3, 0)
    z_step(3, 1)
    with scope("k2"):
        rs_k.second()
    z_block(1)
    with scope("q4"):
        rs_q.fourth()
    z_step(2, 0)
    z_step(2, 1)
    with scope("v3"):
        rs_v.third()
    with scope("k3"):
        rs_k.third()
    last = input_block(z)
    z_step(1, 0)
    z_step(1, 1)
    with scope("v4"):
        rs_v.fourth()
    with scope("k4"):
        rs_k.fourth()
    with scope("q5"):
        rs_q.finish(dq_out)
    with scope("v5"):
        rs_v.finish(dv_out)
    with scope("k5"):
        rs_k.finish(dk_out)
    with scope("zlast"):
        for copies in zs:
            for copy in copies:
                copy.wait_recv()
        dx_out[...] = (last + zr[0, 3].astype(F32) + zr[1, 3].astype(F32)).astype(BF16)
    for copy in started:
        copy.wait_send()


def publish(a, b, c, d, oa, ob, oc, od):
    for src, dst in ((a, oa), (b, ob), (c, oc), (d, od)):
        dst[...] = src[...]


def body(normed, queries, keys, values, grads, links, wq, wk, wv):
    length, cols = queries.shape[2:]
    width = normed.shape[-1]
    heads = cols // HD
    rows = wq.shape[0]
    vmem = pl.BlockSpec(memory_space=pltpu.VMEM)
    anywhere = pl.BlockSpec(memory_space=pl.ANY)
    count = 144
    out = pl.pallas_call(
        kernel,
        out_shape=(
            jax.ShapeDtypeStruct((length, cols), BF16),
            jax.ShapeDtypeStruct((rows, cols), F32),
            jax.ShapeDtypeStruct((rows, cols), F32),
            jax.ShapeDtypeStruct((rows, cols), F32),
        ),
        in_specs=[pl.BlockSpec(memory_space=pltpu.SMEM)] + [anywhere] * 8,
        out_specs=(vmem,) * 4,
        scratch_shapes=[
            pltpu.VMEM((length, width), BF16),
            *[pltpu.VMEM((length, cols), BF16)] * 4,
            pltpu.VMEM((2, 2, heads, length, HD), BF16),
            pltpu.VMEM((4, 2, 2, 2, rows, 3 * cols), BF16),
            pltpu.VMEM((4, 2, 2, 2, rows, length), BF16),
            pltpu.VMEM((4, 2, 2, rows, length), BF16),
            pltpu.VMEM((length, 3 * cols), BF16),
            pltpu.VMEM((length, 3 * cols), BF16),
            pltpu.VMEM((heads, 2, length, HD), F32),
            pltpu.VMEM((2, heads, 2, length, HD), BF16),
            pltpu.VMEM((2, heads, 2, length, HD), BF16),
            pltpu.VMEM((3, 4, 4, rows, cols), BF16),
            pltpu.VMEM((3, 2, 2, rows, cols), BF16),
            pltpu.VMEM((3, 2, 4, rows, cols), BF16),
            pltpu.VMEM((3, 4, rows, cols), BF16),
            pltpu.VMEM((3, 2, rows // 2, cols), BF16),
            pltpu.VMEM((3, 2, rows, cols), BF16),
            pltpu.VMEM((8, length, cols), BF16),
            pltpu.VMEM((2, 4, length, cols), BF16),
            pltpu.SemaphoreType.DMA((count,)),
            pltpu.SemaphoreType.DMA((count,)),
            pltpu.SemaphoreType.DMA((8,)),
        ],
        compiler_params=pltpu.CompilerParams(
            collective_id=0, has_side_effects=True, vmem_limit_bytes=56 * 1024 * 1024
        ),
        name="attention_backward",
    )(
        links,
        normed.reshape(length, width),
        *(value.reshape(length, cols) for value in (queries, keys, values, grads)),
        wq, wk, wv,
    )
    out = pl.pallas_call(
        publish,
        out_shape=[jax.ShapeDtypeStruct(o.shape, o.dtype) for o in out],
        in_specs=[vmem] * 4,
        out_specs=[vmem] * 4,
        name="publish",
    )(*out)
    return (out[0].reshape(1, 1, length, cols), out[1], out[2], out[3])


def solution(mesh):
    tokens = P("dp", "view", None, "head")
    weight = P(("dp", "view"), "head")
    return jax.shard_map(
        body,
        mesh=mesh,
        in_specs=(P("dp", "view", None, None),) + (tokens,) * 4 + (P("view", None),) + (weight,) * 3,
        out_specs=(tokens,) + (weight,) * 3,
        check_vma=False,
    )
```

```python
import contextlib

import jax
import jax.numpy as jnp
from jax import lax
from jax.experimental import pallas as pl
from jax.experimental.pallas import tpu as pltpu
from jax.sharding import PartitionSpec as P

HD = 128
SPLIT = 64
MESH = pl.DeviceIdType.MESH
F32 = jnp.float32
BF16 = jnp.bfloat16
NT = (((1,), (1,)), ((), ()))
NN = (((1,), (0,)), ((), ()))
TN = (((0,), (0,)), ((), ()))


def scope(name):
    return contextlib.nullcontext()


def dot(a, b, dims):
    return lax.dot_general(a, b, dims, preferred_element_type=F32)


def kernel(
    links, n_hbm, q_hbm, k_hbm, v_hbm, g_hbm, wq, wk, wv,
    dx_out, dq_out, dk_out, dv_out,
    normed, q_ref, k_ref, v_ref, g_ref,
    kv, wg, nt, ntp, hown, hpar, own, gs, gr, part, ra1, rra, rb, rb1, rrb, zb, zr,
    ssem, rsem, lsem,
):
    length, cols = q_ref.shape
    heads = cols // HD
    rows = wq.shape[0]
    half = rows // 2
    scaling = HD ** (-0.5)
    dp, vw, z = lax.axis_index("dp"), lax.axis_index("view"), lax.axis_index("head")
    nview, nz = 16, 8
    x = lax.div(vw, 4)
    yh = lax.rem(lax.div(vw, 2), 2)
    c = lax.rem(vw, 2)
    y = yh * 2 + dp

    def at(xx, yy, cc, zz):
        return (lax.rem(yy, 2), xx * 4 + lax.div(yy, 2) * 2 + cc, zz)

    def m(value, n):
        return lax.rem(value + 2 * n, n)

    x_up, x_dn, x_far = m(x + 1, 4), m(x - 1, 4), m(x + 2, 4)
    y_up, y_dn = m(y + 1, 4), m(y - 1, 4)
    to_x = {1: at(x_up, y, c, z), -1: at(x_dn, y, c, z)}
    to_y = {1: at(x, y_up, c, z), -1: at(x, y_dn, c, z)}
    to_z = {1: (dp, vw, m(z + 1, nz)), -1: (dp, vw, m(z - 1, nz))}
    to_view = {1: (dp, m(vw + 1, nview), z), -1: (dp, m(vw - 1, nview), z)}
    partner = at(x, y, 1 - c, z)

    started = []

    def send(src, dst, device):
        slot = len(started)
        copy = pltpu.make_async_remote_copy(
            src_ref=src, dst_ref=dst, send_sem=ssem.at[slot], recv_sem=rsem.at[slot],
            device_id=device, device_id_type=MESH,
        )
        copy.start()
        started.append(copy)
        return copy

    barrier = pltpu.get_barrier_semaphore()
    for peers in (to_view, to_x, to_y, to_z):
        for step in (1, -1):
            pl.semaphore_signal(barrier, inc=1, device_id=peers[step], device_id_type=MESH)
    yl = dp

    def load(src, dst, slot):
        copy = pltpu.make_async_copy(src, dst, lsem.at[slot])
        copy.start()
        return copy

    w_loads = [
        load(w, wg.at[x, yl, yh, c, :, pl.ds(i * cols, cols)], i)
        for i, w in enumerate((wq, wk, wv))
    ]
    kv_loads = [load(k_hbm, k_ref, 3), load(v_hbm, v_ref, 4)]
    loads = [load(q_hbm, q_ref, 5), load(g_hbm, g_ref, 6), load(n_hbm, normed, 7)]
    for copy in w_loads + kv_loads:
        copy.wait()
    with scope("barrier"):
        pl.semaphore_wait(barrier, 8)

    turn = 1 - 2 * yh
    to_turn = at(m(x + turn, 4), y, c, z)

    class Gather:
        def __init__(self, start, size, x_first):
            self.x_first = x_first
            self.all = pl.ds(start, size)
            self.to_a, self.to_b = (to_x, to_y) if x_first else (to_y, to_x)
            self.half = (pl.ds(start, size // 2), pl.ds(start + size // 2, size // 2))
            side = size // 4
            self.outer = (pl.ds(start, side), pl.ds(start + size - side, side))
            self.inner = pl.ds(start + side, size - 2 * side)
            self.b1, self.b2, self.par, self.tail = {}, {}, {}, []

        def ref(self, ao, bo, piece):
            xo, yo = (ao, bo) if self.x_first else (bo, ao)
            yy = m(y + yo, 4)
            return wg.at[m(x + xo, 4), lax.rem(yy, 2), lax.div(yy, 2), c, piece]

        def pass_on(self, ao, bo, piece, device):
            block = self.ref(ao, bo, piece)
            return send(block, block, device)

        def start(self):
            self.a1 = [self.pass_on(0, 0, self.all, self.to_a[s]) for s in (1, -1)]

        def across(self, ao):
            self.b1[ao] = [self.pass_on(ao, 0, self.all, self.to_b[s]) for s in (1, -1)]

        def forward(self):
            for copy in self.a1:
                copy.wait_recv()
            if self.x_first:
                self.a2 = [self.pass_on(-turn, 0, self.all, to_turn)]
            else:
                self.a2 = [self.pass_on(-s, 0, self.half[i], self.to_a[s]) for i, s in enumerate((1, -1))]

        def far(self):
            for copy in self.a2:
                copy.wait_recv()

        def across_forward(self, ao):
            for copy in self.b1[ao]:
                copy.wait_recv()
            if self.x_first:
                self.b2[ao] = [self.pass_on(ao, -s, self.half[i], self.to_b[s]) for i, s in enumerate((1, -1))]
            else:
                self.b2[ao] = [self.pass_on(ao, -s, self.outer[i], self.to_b[s]) for i, s in enumerate((1, -1))]
                self.b2[ao].append(self.pass_on(ao, -turn, self.inner, to_turn))

        def across_far(self, ao):
            for copy in self.b2[ao]:
                copy.wait_recv()
            self.tail.append(self.pass_on(ao, 2, self.all, partner))

        def to_partner(self, bo):
            if self.x_first:
                yy = m(y + bo, 4)
                block = wg.at[:, lax.rem(yy, 2), lax.div(yy, 2), c, self.all]
            else:
                block = wg.at[m(x + bo, 4), :, :, c, self.all]
            self.par[bo] = send(block, block, partner)

    ga = Gather(0, SPLIT, False)
    gb = Gather(SPLIT, rows - SPLIT, True)
    ga.start()
    gb.start()
    ga.across(0)
    halo = []
    for h in range(heads):
        hs = pl.ds(h * HD, HD)
        copies = []
        for slot, step in ((0, 1), (1, -1)):
            copies.append(send(k_ref.at[:, hs], kv.at[slot, 0, h], to_view[step]))
            copies.append(send(v_ref.at[:, hs], kv.at[slot, 1, h], to_view[step]))
        halo.append(copies)
    gb.across(0)
    for copy in loads:
        copy.wait()
    lo, hi = pl.ds(0, half), pl.ds(half, half)

    def transpose_chunk(i, _):
        chunk = normed[:, pl.ds(pl.multiple_of(i * 4 * rows, 128), 4 * rows)]
        turned = chunk.T.reshape(2, 2, rows, length)
        nt[lax.rem(i, 4), lax.div(i, 4)] = turned
        return 0

    with scope("transpose"):
        lax.fori_loop(0, 8, transpose_chunk, 0)
    with scope("gb_forward"):
        gb.forward()
    with scope("ga_forward"):
        ga.forward()
        ga.across(-1)
        ga.across(1)
    gb.across(-1)
    gb.across(1)
    turned_copy = send(nt.at[:, :, :, 1 - c], ntp, partner)
    with scope("ga_af0"):
        ga.across_forward(0)

    pen = [
        jnp.where(links[0, 0] >= 0, 0.0, -1e30).astype(F32),
        None,
        jnp.where(links[0, 1] >= 0, 0.0, -1e30).astype(F32),
    ]
    grad_halo = []
    w_x1, w_x2, w_par = [], [], []

    def attention(h):
        hs = slice(h * HD, (h + 1) * HD)
        for copy in halo[h]:
            copy.wait_recv()
        qh, gh = q_ref[:, hs], g_ref[:, hs]
        ks = [kv[0, 0, h], k_ref[:, hs], kv[1, 0, h]]
        vs = [kv[0, 1, h], v_ref[:, hs], kv[1, 1, h]]
        scores = []
        for j in range(3):
            s = dot(qh, ks[j], NT) * scaling
            scores.append(s if pen[j] is None else s + pen[j])
        top = jnp.maximum(jnp.maximum(scores[0], scores[1]), scores[2])
        top = jnp.max(top, axis=-1, keepdims=True)
        powers = [jnp.exp(s - top) for s in scores]
        total = jnp.sum(powers[0] + powers[1] + powers[2], axis=-1, keepdims=True)
        inv = 1.0 / total
        probs = [e * inv for e in powers]
        pgrads = [dot(gh, vj, NT) for vj in vs]
        delta = probs[0] * pgrads[0] + probs[1] * pgrads[1] + probs[2] * pgrads[2]
        delta = jnp.sum(delta, axis=-1, keepdims=True)
        sg = [(scaling * p * (d - delta)).astype(BF16) for p, d in zip(probs, pgrads)]
        query = dot(sg[0], ks[0], NN) + dot(sg[1], ks[1], NN) + dot(sg[2], ks[2], NN)
        hown[:, hs] = query.astype(BF16)
        for j, slot in ((0, 0), (2, 1)):
            gs[slot, h, 0] = dot(sg[j], qh, TN).astype(BF16)
            gs[slot, h, 1] = dot(probs[j].astype(BF16), gh, TN).astype(BF16)
        own[h, 0] = dot(sg[1], qh, TN)
        own[h, 1] = dot(probs[1].astype(BF16), gh, TN)
        grad_halo.append(
            [
                send(gs.at[0, h], gr.at[0, h], to_view[-1]),
                send(gs.at[1, h], gr.at[1, h], to_view[1]),
            ]
        )

    for h in range(heads):
        with scope("att"):
            attention(h)
    hq = hown.at[:, pl.ds(0, cols)]
    q_copy = send(hq, hpar.at[:, pl.ds(0, cols)], partner)
    with scope("ga_far"):
        ga.far()
        ga.across(2)
        ga.to_partner(0)
    with scope("gb_far"):
        gb.far()
        gb.across(2)
        gb.to_partner(0)
    with scope("ga_af1"):
        ga.across_forward(-1)
        ga.across_forward(1)
    def weight_part(ci, x_first):
        cs = slice(ci * cols, (ci + 1) * cols)

        def step(xx, _):
            a = nt[xx, :, :, c].reshape(4 * rows, length)
            b = ntp[xx].reshape(4 * rows, length)
            acc = dot(a, hown[:, cs], NN) + dot(b, hpar[:, cs], NN)
            acc = acc.astype(BF16)
            for ll in range(2):
                for hh in range(2):
                    yy, start = hh * 2 + ll, (ll * 2 + hh) * rows
                    block = acc[start : start + rows]
                    if x_first:
                        part[ci, xx, yy] = block
                    else:
                        part[ci, yy, xx] = block
            return 0

        lax.fori_loop(0, 4, step, 0)

    class Scatter:
        def __init__(self, ci, pa, to_a, pb, to_b):
            self.ci, self.pa, self.to_a, self.pb, self.to_b = ci, pa, to_a, pb, to_b
            self.aup, self.adn, self.afar = m(pa + 1, 4), m(pa - 1, 4), m(pa + 2, 4)
            self.bup, self.bdn, self.bfar = m(pb + 1, 4), m(pb - 1, 4), m(pb + 2, 4)

        def first(self):
            ci = self.ci
            low, high = pl.ds(0, 2), pl.ds(2, 2)
            self.f1 = [
                send(part.at[ci, self.afar, low], ra1.at[ci, 0], self.to_a[1]),
                send(part.at[ci, self.afar, high], ra1.at[ci, 1], self.to_a[-1]),
            ]
            self.f2 = [
                send(part.at[ci, self.aup, high], rra.at[ci, 0, high], self.to_a[1]),
                send(part.at[ci, self.adn, low], rra.at[ci, 1, low], self.to_a[-1]),
            ]

        def second(self):
            ci = self.ci
            low, high = pl.ds(0, 2), pl.ds(2, 2)
            for i, (block, piece, device) in enumerate(
                ((self.aup, low, self.to_a[1]), (self.adn, high, self.to_a[-1]))
            ):
                self.f1[i].wait_recv()
                old = part[ci, block, piece].astype(F32)
                part[ci, block, piece] = (old + ra1[ci, i].astype(F32)).astype(BF16)
                self.f2.append(send(part.at[ci, block, piece], rra.at[ci, i, piece], device))

        def third(self):
            ci = self.ci
            for copy in self.f2:
                copy.wait_recv()
            for j in range(4):
                value = part[ci, self.pa, j].astype(F32) + rra[ci, 0, j].astype(F32)
                rb[ci, j] = (value + rra[ci, 1, j].astype(F32)).astype(BF16)
            self.g1 = [
                send(rb.at[ci, self.bfar, lo], rb1.at[ci, 0], self.to_b[1]),
                send(rb.at[ci, self.bfar, hi], rb1.at[ci, 1], self.to_b[-1]),
            ]
            self.g2 = [
                send(rb.at[ci, self.bup, hi], rrb.at[ci, 0, hi], self.to_b[1]),
                send(rb.at[ci, self.bdn, lo], rrb.at[ci, 1, lo], self.to_b[-1]),
            ]

        def fourth(self):
            ci = self.ci
            for i, (block, piece, device) in enumerate(
                ((self.bup, lo, self.to_b[1]), (self.bdn, hi, self.to_b[-1]))
            ):
                self.g1[i].wait_recv()
                old = rb[ci, block, piece].astype(F32)
                rb[ci, block, piece] = (old + rb1[ci, i].astype(F32)).astype(BF16)
                self.g2.append(send(rb.at[ci, block, piece], rrb.at[ci, i, piece], device))

        def finish(self, out):
            ci = self.ci
            for copy in self.g2:
                copy.wait_recv()
            value = rb[ci, self.pb].astype(F32) + rrb[ci, 0].astype(F32)
            out[...] = (value + rrb[ci, 1].astype(F32)) * (1.0 / 32.0)

    rs_q = Scatter(0, x, to_x, y, to_y)
    rs_k = Scatter(1, x, to_x, y, to_y)
    rs_v = Scatter(2, y, to_y, x, to_x)

    with scope("wp_q"):
        turned_copy.wait_recv()
        q_copy.wait_recv()
        weight_part(0, True)
    with scope("ga_af2"):
        ga.across_forward(2)
        ga.to_partner(-1)
        ga.to_partner(1)
    rs_q.first()
    with scope("ga_bf0"):
        ga.across_far(0)
    with scope("gb_af1"):
        gb.across_forward(0)
        gb.across_forward(-1)
        gb.across_forward(1)
    with scope("gh_wait"):
        for h in range(heads):
            for copy in grad_halo[h]:
                copy.wait_recv()
            for i in range(2):
                value = own[h, i] + gr[0, h, i].astype(F32) + gr[1, h, i].astype(F32)
                start = (1 + i) * cols + h * HD
                hown[:, start : start + HD] = value.astype(BF16)
    hkv = pl.ds(cols, 2 * cols)
    kv_copy = send(hown.at[:, hkv], hpar.at[:, hkv], partner)
    with scope("gb_af2"):
        gb.across_forward(2)
        gb.to_partner(-1)
        gb.to_partner(1)
    with scope("ga_bf1"):
        ga.across_far(-1)
        ga.across_far(1)
    with scope("wp_v"):
        kv_copy.wait_recv()
        weight_part(2, False)
    rs_v.first()
    with scope("ga_bf"):
        ga.across_far(2)
    with scope("gb_bf"):
        for ao in (0, -1, 1, 2):
            gb.across_far(ao)
    with scope("wpar"):
        for group in (ga, gb):
            for copy in list(group.par.values()) + group.tail:
                copy.wait_recv()

    def input_block(j):
        w = wg[lax.rem(j, 4), lax.div(j, 4)].reshape(4 * rows, 3 * cols)
        return dot(hown[...], w, NT)

    part_rows = length // 2
    half_rows = part_rows // 2
    far = m(z + 4, nz)
    with scope("zfar"):
        zb[far] = input_block(far).astype(BF16)
    zs = [[], []]
    for p in range(2):
        for i, sign in ((0, 1), (1, -1)):
            piece = pl.ds(p * part_rows + i * half_rows, half_rows)
            zs[p].append(send(zb.at[far, piece], zr.at[i, 0, piece], to_z[sign]))

    def z_block(step):
        with scope("zb"):
            for sign in (1, -1):
                j = m(z + sign * step, nz)
                zb[j] = input_block(j).astype(BF16)

    def z_step(step, p):
        with scope("z%d%d" % (step, p)):
            new = []
            whole = pl.ds(p * part_rows, part_rows)
            for i, sign in ((0, 1), (1, -1)):
                piece = pl.ds(p * part_rows + i * half_rows, half_rows) if step == 3 else whole
                j = m(z + sign * step, nz)
                zs[p][i].wait_recv()
                value = zb[j, piece].astype(F32) + zr[i, 3 - step, piece].astype(F32)
                zb[j, piece] = value.astype(BF16)
                new.append(send(zb.at[j, whole], zr.at[i, 4 - step, whole], to_z[sign]))
            zs[p] = new

    with scope("wp_k"):
        weight_part(1, True)
    with scope("q2"):
        rs_q.second()
    rs_k.first()
    z_block(3)
    z_step(3, 0)
    z_step(3, 1)
    with scope("v2"):
        rs_v.second()
    z_block(2)
    with scope("q3"):
        rs_q.third()
    z_step(2, 0)
    z_step(2, 1)
    with scope("k2"):
        rs_k.second()
    z_block(1)
    with scope("v3"):
        rs_v.third()
    z_step(1, 0)
    with scope("q4"):
        rs_q.fourth()
    z_step(1, 1)
    last = input_block(z)
    with scope("k3"):
        rs_k.third()
    with scope("v4"):
        rs_v.fourth()
    with scope("k4"):
        rs_k.fourth()
    with scope("q5"):
        rs_q.finish(dq_out)
    with scope("v5"):
        rs_v.finish(dv_out)
    with scope("zlast"):
        for copies in zs:
            for copy in copies:
                copy.wait_recv()
        dx_out[...] = (last + zr[0, 3].astype(F32) + zr[1, 3].astype(F32)).astype(BF16)
    with scope("k5"):
        rs_k.finish(dk_out)
    for copy in started:
        copy.wait_send()


def publish(a, b, c, d, oa, ob, oc, od):
    for src, dst in ((a, oa), (b, ob), (c, oc), (d, od)):
        dst[...] = src[...]


def body(normed, queries, keys, values, grads, links, wq, wk, wv):
    length, cols = queries.shape[2:]
    width = normed.shape[-1]
    heads = cols // HD
    rows = wq.shape[0]
    vmem = pl.BlockSpec(memory_space=pltpu.VMEM)
    anywhere = pl.BlockSpec(memory_space=pl.ANY)
    count = 176
    out = pl.pallas_call(
        kernel,
        out_shape=(
            jax.ShapeDtypeStruct((length, cols), BF16),
            jax.ShapeDtypeStruct((rows, cols), F32),
            jax.ShapeDtypeStruct((rows, cols), F32),
            jax.ShapeDtypeStruct((rows, cols), F32),
        ),
        in_specs=[pl.BlockSpec(memory_space=pltpu.SMEM)] + [anywhere] * 8,
        out_specs=(vmem,) * 4,
        scratch_shapes=[
            pltpu.VMEM((length, width), BF16),
            *[pltpu.VMEM((length, cols), BF16)] * 4,
            pltpu.VMEM((2, 2, heads, length, HD), BF16),
            pltpu.VMEM((4, 2, 2, 2, rows, 3 * cols), BF16),
            pltpu.VMEM((4, 2, 2, 2, rows, length), BF16),
            pltpu.VMEM((4, 2, 2, rows, length), BF16),
            pltpu.VMEM((length, 3 * cols), BF16),
            pltpu.VMEM((length, 3 * cols), BF16),
            pltpu.VMEM((heads, 2, length, HD), F32),
            pltpu.VMEM((2, heads, 2, length, HD), BF16),
            pltpu.VMEM((2, heads, 2, length, HD), BF16),
            pltpu.VMEM((3, 4, 4, rows, cols), BF16),
            pltpu.VMEM((3, 2, 2, rows, cols), BF16),
            pltpu.VMEM((3, 2, 4, rows, cols), BF16),
            pltpu.VMEM((3, 4, rows, cols), BF16),
            pltpu.VMEM((3, 2, rows // 2, cols), BF16),
            pltpu.VMEM((3, 2, rows, cols), BF16),
            pltpu.VMEM((8, length, cols), BF16),
            pltpu.VMEM((2, 4, length, cols), BF16),
            pltpu.SemaphoreType.DMA((count,)),
            pltpu.SemaphoreType.DMA((count,)),
            pltpu.SemaphoreType.DMA((8,)),
        ],
        compiler_params=pltpu.CompilerParams(
            collective_id=0, has_side_effects=True, vmem_limit_bytes=56 * 1024 * 1024
        ),
        name="attention_backward",
    )(
        links,
        normed.reshape(length, width),
        *(value.reshape(length, cols) for value in (queries, keys, values, grads)),
        wq, wk, wv,
    )
    out = pl.pallas_call(
        publish,
        out_shape=[jax.ShapeDtypeStruct(o.shape, o.dtype) for o in out],
        in_specs=[vmem] * 4,
        out_specs=[vmem] * 4,
        name="publish",
    )(*out)
    return (out[0].reshape(1, 1, length, cols), out[1], out[2], out[3])


def solution(mesh):
    tokens = P("dp", "view", None, "head")
    weight = P(("dp", "view"), "head")
    return jax.shard_map(
        body,
        mesh=mesh,
        in_specs=(P("dp", "view", None, None),) + (tokens,) * 4 + (P("view", None),) + (weight,) * 3,
        out_specs=(tokens,) + (weight,) * 3,
        check_vma=False,
    )
```

```python
import contextlib

import jax
import jax.numpy as jnp
from jax import lax
from jax.experimental import pallas as pl
from jax.experimental.pallas import tpu as pltpu
from jax.sharding import PartitionSpec as P

HD = 128
SPLIT = 64
MESH = pl.DeviceIdType.MESH
F32 = jnp.float32
BF16 = jnp.bfloat16
NT = (((1,), (1,)), ((), ()))
NN = (((1,), (0,)), ((), ()))
TN = (((0,), (0,)), ((), ()))


def scope(name):
    return contextlib.nullcontext()


def dot(a, b, dims):
    return lax.dot_general(a, b, dims, preferred_element_type=F32)


def kernel(
    links, n_hbm, q_hbm, k_hbm, v_hbm, g_hbm, wq, wk, wv,
    dx_hbm, dq_hbm, dk_hbm, dv_hbm,
    dx_out, dq_out, dk_out, dv_out,
    normed, q_ref, k_ref, v_ref, g_ref,
    relay, kv, wg, nt, ntp, hown, hpar, own, gs, gr, part, ra1, rra, rb, rrb, zb, zr,
    ssem, rsem, lsem,
):
    length, cols = q_ref.shape
    heads = cols // HD
    rows = wq.shape[0]
    half = rows // 2
    scaling = HD ** (-0.5)
    dp, vw, z = lax.axis_index("dp"), lax.axis_index("view"), lax.axis_index("head")
    nz = 8
    x = lax.div(vw, 4)
    yh = lax.rem(lax.div(vw, 2), 2)
    c = lax.rem(vw, 2)
    y = yh * 2 + dp

    def at(xx, yy, cc, zz):
        return (lax.rem(yy, 2), xx * 4 + lax.div(yy, 2) * 2 + cc, zz)

    def m(value, n):
        return lax.rem(value + 2 * n, n)

    x_up, x_dn, x_far = m(x + 1, 4), m(x - 1, 4), m(x + 2, 4)
    y_up, y_dn = m(y + 1, 4), m(y - 1, 4)
    to_x = {1: at(x_up, y, c, z), -1: at(x_dn, y, c, z)}
    to_y = {1: at(x, y_up, c, z), -1: at(x, y_dn, c, z)}
    to_z = {1: (dp, vw, m(z + 1, nz)), -1: (dp, vw, m(z - 1, nz))}
    partner = at(x, y, 1 - c, z)

    def cross(yy):
        upper = lax.div(yy, 2)
        return c * upper - (1 - c) * (1 - upper)

    def outward(yy):
        return at(m(x + cross(yy), 4), m(yy + 2, 4), 1 - c, z)

    over = (outward(m(y - 1, 4)), outward(m(y + 1, 4)))

    started = []

    def send(src, dst, device):
        slot = len(started)
        copy = pltpu.make_async_remote_copy(
            src_ref=src, dst_ref=dst, send_sem=ssem.at[slot], recv_sem=rsem.at[slot],
            device_id=device, device_id_type=MESH,
        )
        copy.start()
        started.append(copy)
        return copy

    barrier = pltpu.get_barrier_semaphore()
    peers = [partner, at(x_far, y, c, z), at(x, m(y + 2, 4), c, z)]
    for ring in (to_x, to_y, to_z):
        peers += [ring[1], ring[-1]]
    peers += [at(m(x + cross(y), 4), m(y + s, 4), 1 - c, z) for s in (1, -1)]
    for peer in peers:
        pl.semaphore_signal(barrier, inc=1, device_id=peer, device_id_type=MESH)
    yl = dp

    def load(src, dst, slot):
        copy = pltpu.make_async_copy(src, dst, lsem.at[slot])
        copy.start()
        return copy

    stored = []

    def put(src, dst, slot):
        stored.append(load(src, dst, slot))

    w_loads = [
        load(w, wg.at[x, yl, yh, c, :, pl.ds(i * cols, cols)], i)
        for i, w in enumerate((wq, wk, wv))
    ]
    kv_loads = [load(k_hbm, k_ref, 3), load(v_hbm, v_ref, 4)]
    loads = [load(q_hbm, q_ref, 5), load(g_hbm, g_ref, 6), load(n_hbm, normed, 7)]
    for copy in w_loads + kv_loads:
        copy.wait()
    with scope("barrier"):
        pl.semaphore_wait(barrier, len(peers))

    turn = 1 - 2 * yh
    to_turn = at(m(x + turn, 4), y, c, z)

    class Gather:
        def __init__(self, start, size, x_first):
            self.x_first = x_first
            self.all = pl.ds(start, size)
            self.to_a, self.to_b = (to_x, to_y) if x_first else (to_y, to_x)
            self.half = (pl.ds(start, size // 2), pl.ds(start + size // 2, size // 2))
            side = size // 4
            self.outer = (pl.ds(start, side), pl.ds(start + size - side, side))
            self.inner = pl.ds(start + side, size - 2 * side)
            self.b1, self.b2, self.par, self.tail = {}, {}, {}, []

        def ref(self, ao, bo, piece):
            xo, yo = (ao, bo) if self.x_first else (bo, ao)
            yy = m(y + yo, 4)
            return wg.at[m(x + xo, 4), lax.rem(yy, 2), lax.div(yy, 2), c, piece]

        def pass_on(self, ao, bo, piece, device):
            block = self.ref(ao, bo, piece)
            return send(block, block, device)

        def start(self):
            self.a1 = [self.pass_on(0, 0, self.all, self.to_a[s]) for s in (1, -1)]

        def across(self, ao):
            self.b1[ao] = [self.pass_on(ao, 0, self.all, self.to_b[s]) for s in (1, -1)]

        def forward(self):
            for copy in self.a1:
                copy.wait_recv()
            if self.x_first:
                self.a2 = [self.pass_on(-turn, 0, self.all, to_turn)]
            else:
                self.a2 = [self.pass_on(-s, 0, self.half[i], self.to_a[s]) for i, s in enumerate((1, -1))]

        def far(self):
            for copy in self.a2:
                copy.wait_recv()

        def across_forward(self, ao):
            for copy in self.b1[ao]:
                copy.wait_recv()
            if self.x_first:
                self.b2[ao] = [self.pass_on(ao, -s, self.half[i], self.to_b[s]) for i, s in enumerate((1, -1))]
            else:
                self.b2[ao] = [self.pass_on(ao, -s, self.outer[i], self.to_b[s]) for i, s in enumerate((1, -1))]
                self.b2[ao].append(self.pass_on(ao, -turn, self.inner, to_turn))

        def across_far(self, ao):
            for copy in self.b2[ao]:
                copy.wait_recv()
            self.tail.append(self.pass_on(ao, 2, self.all, partner))

        def to_partner(self, bo):
            if self.x_first:
                yy = m(y + bo, 4)
                block = wg.at[:, lax.rem(yy, 2), lax.div(yy, 2), c, self.all]
            else:
                block = wg.at[m(x + bo, 4), :, :, c, self.all]
            self.par[bo] = send(block, block, partner)

    ga = Gather(0, SPLIT, False)
    gb = Gather(SPLIT, rows - SPLIT, True)
    ga.start()
    gb.start()
    ga.across(0)
    halo, hops = [], []
    for h in range(heads):
        hs = pl.ds(h * HD, HD)
        pair = (k_ref.at[:, hs], v_ref.at[:, hs])
        halo.append([send(pair[i], kv.at[c, i, h], partner) for i in range(2)])
        hops.append([send(pair[i], relay.at[0, i, h], to_y[s]) for i, s in enumerate((1, -1))])
    for copy in loads:
        copy.wait()
    lo, hi = pl.ds(0, half), pl.ds(half, half)

    def transpose_chunk(i, _):
        chunk = normed[:, pl.ds(pl.multiple_of(i * 4 * rows, 128), 4 * rows)]
        turned = chunk.T.reshape(2, 2, rows, length)
        nt[lax.rem(i, 4), lax.div(i, 4)] = turned
        return 0

    with scope("transpose"):
        lax.fori_loop(0, 8, transpose_chunk, 0)
    with scope("gb_forward"):
        gb.forward()
    with scope("ga_forward"):
        ga.forward()
        ga.across(-1)
        ga.across(1)
    for h in range(heads):
        with scope("relay%d" % h):
            for i in range(2):
                hops[h][i].wait_recv()
                halo[h].append(send(relay.at[0, i, h], kv.at[1 - c, i, h], over[i]))
    gb.across(0)
    gb.across(-1)
    gb.across(1)
    turned_copy = send(nt.at[:, :, :, 1 - c], ntp, partner)
    with scope("ga_af0"):
        ga.across_forward(0)
    with scope("ga_far"):
        ga.far()
        ga.across(2)
        ga.to_partner(0)

    pen = [
        jnp.where(links[0, 0] >= 0, 0.0, -1e30).astype(F32),
        None,
        jnp.where(links[0, 1] >= 0, 0.0, -1e30).astype(F32),
    ]
    grad_halo, grad_hops = [], []
    w_x1, w_x2, w_par = [], [], []

    def attention(h):
        hs = slice(h * HD, (h + 1) * HD)
        for copy in halo[h]:
            copy.wait_recv()
        qh, gh = q_ref[:, hs], g_ref[:, hs]
        ks = [kv[0, 0, h], k_ref[:, hs], kv[1, 0, h]]
        vs = [kv[0, 1, h], v_ref[:, hs], kv[1, 1, h]]
        scores = []
        for j in range(3):
            s = dot(qh, ks[j], NT) * scaling
            scores.append(s if pen[j] is None else s + pen[j])
        top = jnp.maximum(jnp.maximum(scores[0], scores[1]), scores[2])
        top = jnp.max(top, axis=-1, keepdims=True)
        powers = [jnp.exp(s - top) for s in scores]
        total = jnp.sum(powers[0] + powers[1] + powers[2], axis=-1, keepdims=True)
        inv = 1.0 / total
        probs = [e * inv for e in powers]
        pgrads = [dot(gh, vj, NT) for vj in vs]
        delta = probs[0] * pgrads[0] + probs[1] * pgrads[1] + probs[2] * pgrads[2]
        delta = jnp.sum(delta, axis=-1, keepdims=True)
        sg = [(scaling * p * (d - delta)).astype(BF16) for p, d in zip(probs, pgrads)]
        query = dot(sg[0], ks[0], NN) + dot(sg[1], ks[1], NN) + dot(sg[2], ks[2], NN)
        hown[:, hs] = query.astype(BF16)
        for j, slot in ((0, 0), (2, 1)):
            gs[slot, h, 0] = dot(sg[j], qh, TN).astype(BF16)
            gs[slot, h, 1] = dot(probs[j].astype(BF16), gh, TN).astype(BF16)
        own[h, 0] = dot(sg[1], qh, TN)
        own[h, 1] = dot(probs[1].astype(BF16), gh, TN)
        grad_halo.append([send(gs.at[1 - c, h], gr.at[0, h], partner)])
        grad_hops.append(
            [send(gs.at[c, h, i], relay.at[1, i, h], to_y[s]) for i, s in enumerate((1, -1))]
        )

    def grad_relay(h):
        with scope("gr%d" % h):
            for i in range(2):
                grad_hops[h][i].wait_recv()
                grad_halo[h].append(send(relay.at[1, i, h], gr.at[1, h, i], over[i]))

    for h in range(heads):
        with scope("att"):
            attention(h)
    hq = hown.at[:, pl.ds(0, cols)]
    q_copy = send(hq, hpar.at[:, pl.ds(0, cols)], partner)
    with scope("ga_af1"):
        ga.across_forward(-1)
        ga.across_forward(1)
    grad_relay(0)
    grad_relay(1)
    with scope("gb_far"):
        gb.far()
        gb.across(2)
        gb.to_partner(0)

    def weight_part(first, *orders):
        cs = slice(first * cols, (first + len(orders)) * cols)

        def step(xx, _):
            a = nt[xx, :, :, c].reshape(4 * rows, length)
            b = ntp[xx].reshape(4 * rows, length)
            acc = dot(a, hown[:, cs], NN) + dot(b, hpar[:, cs], NN)
            acc = acc.astype(BF16)
            for i, x_first in enumerate(orders):
                for ll in range(2):
                    for hh in range(2):
                        yy, start = hh * 2 + ll, (ll * 2 + hh) * rows
                        block = acc[start : start + rows, i * cols : (i + 1) * cols]
                        if x_first:
                            part[first + i, xx, yy] = block
                        else:
                            part[first + i, yy, xx] = block
            return 0

        lax.fori_loop(0, 4, step, 0)

    class Scatter:
        def __init__(self, ci, pa, to_a, pb, to_b, to_far):
            self.ci, self.pa, self.to_a, self.pb, self.to_b = ci, pa, to_a, pb, to_b
            self.to_far = to_far
            self.aup, self.adn, self.afar = m(pa + 1, 4), m(pa - 1, 4), m(pa + 2, 4)
            self.bup, self.bdn, self.bfar = m(pb + 1, 4), m(pb - 1, 4), m(pb + 2, 4)

        def first(self):
            ci = self.ci
            low, high = pl.ds(0, 2), pl.ds(2, 2)
            self.f1 = [
                send(part.at[ci, self.afar, low], ra1.at[ci, 0], self.to_a[1]),
                send(part.at[ci, self.afar, high], ra1.at[ci, 1], self.to_a[-1]),
            ]
            self.f2 = [
                send(part.at[ci, self.aup, high], rra.at[ci, 0, high], self.to_a[1]),
                send(part.at[ci, self.adn, low], rra.at[ci, 1, low], self.to_a[-1]),
            ]

        def second(self):
            ci = self.ci
            low, high = pl.ds(0, 2), pl.ds(2, 2)
            for i, (block, piece, device) in enumerate(
                ((self.aup, low, self.to_a[1]), (self.adn, high, self.to_a[-1]))
            ):
                self.f1[i].wait_recv()
                old = part[ci, block, piece].astype(F32)
                part[ci, block, piece] = (old + ra1[ci, i].astype(F32)).astype(BF16)
                self.f2.append(send(part.at[ci, block, piece], rra.at[ci, i, piece], device))

        def third(self):
            ci = self.ci
            for copy in self.f2:
                copy.wait_recv()
            for j in range(4):
                value = part[ci, self.pa, j].astype(F32) + rra[ci, 0, j].astype(F32)
                rb[ci, j] = (value + rra[ci, 1, j].astype(F32)).astype(BF16)
            self.g2 = [
                send(rb.at[ci, self.bfar], rrb.at[ci, 2], self.to_far),
                send(rb.at[ci, self.bup], rrb.at[ci, 0], self.to_b[1]),
                send(rb.at[ci, self.bdn], rrb.at[ci, 1], self.to_b[-1]),
            ]

        def finish(self, out):
            ci = self.ci
            for copy in self.g2:
                copy.wait_recv()
            value = rb[ci, self.pb].astype(F32) + rrb[ci, 0].astype(F32)
            value = value + rrb[ci, 1].astype(F32) + rrb[ci, 2].astype(F32)
            out[...] = value * (1.0 / 32.0)

    y_far = at(x, m(y + 2, 4), c, z)
    rs_q = Scatter(0, x, to_x, y, to_y, y_far)
    rs_k = Scatter(1, x, to_x, y, to_y, y_far)
    rs_v = Scatter(2, y, to_y, x, to_x, at(x_far, y, c, z))

    with scope("wp_q"):
        turned_copy.wait_recv()
        q_copy.wait_recv()
        weight_part(0, True)
    grad_relay(2)
    with scope("ga_af2"):
        ga.across_forward(2)
        ga.to_partner(-1)
        ga.to_partner(1)
    rs_q.first()
    with scope("ga_bf0"):
        ga.across_far(0)
    with scope("gb_af1"):
        gb.across_forward(0)
        gb.across_forward(-1)
        gb.across_forward(1)
    with scope("gh_wait"):
        for h in range(heads):
            for copy in grad_halo[h]:
                copy.wait_recv()
            for i in range(2):
                value = own[h, i] + gr[0, h, i].astype(F32) + gr[1, h, i].astype(F32)
                start = (1 + i) * cols + h * HD
                hown[:, start : start + HD] = value.astype(BF16)
    hkv = pl.ds(cols, 2 * cols)
    kv_copy = send(hown.at[:, hkv], hpar.at[:, hkv], partner)
    with scope("gb_af2"):
        gb.across_forward(2)
        gb.to_partner(-1)
        gb.to_partner(1)
    with scope("ga_bf1"):
        ga.across_far(-1)
        ga.across_far(1)
    with scope("wp_v"):
        kv_copy.wait_recv()
        weight_part(1, True, False)
    rs_v.first()
    with scope("ga_bf"):
        ga.across_far(2)
    with scope("gb_bf"):
        for ao in (0, -1, 1, 2):
            gb.across_far(ao)
    with scope("q2"):
        rs_q.second()
    rs_k.first()
    with scope("wpar"):
        for group in (ga, gb):
            for copy in list(group.par.values()) + group.tail:
                copy.wait_recv()

    def input_block(j):
        w = wg[lax.rem(j, 4), lax.div(j, 4)].reshape(4 * rows, 3 * cols)
        return dot(hown[...], w, NT)

    part_rows = length // 2
    half_rows = part_rows // 2
    far = m(z + 4, nz)
    with scope("zfar"):
        zb[far] = input_block(far).astype(BF16)
    zs = [[], []]
    for p in range(2):
        for i, sign in ((0, 1), (1, -1)):
            piece = pl.ds(p * part_rows + i * half_rows, half_rows)
            zs[p].append(send(zb.at[far, piece], zr.at[i, 0, piece], to_z[sign]))

    def z_block(step):
        with scope("zb"):
            for sign in (1, -1):
                j = m(z + sign * step, nz)
                zb[j] = input_block(j).astype(BF16)

    def z_step(step, p):
        with scope("z%d%d" % (step, p)):
            new = []
            whole = pl.ds(p * part_rows, part_rows)
            for i, sign in ((0, 1), (1, -1)):
                piece = pl.ds(p * part_rows + i * half_rows, half_rows) if step == 3 else whole
                j = m(z + sign * step, nz)
                zs[p][i].wait_recv()
                value = zb[j, piece].astype(F32) + zr[i, 3 - step, piece].astype(F32)
                zb[j, piece] = value.astype(BF16)
                new.append(send(zb.at[j, whole], zr.at[i, 4 - step, whole], to_z[sign]))
            zs[p] = new

    z_block(3)
    z_step(3, 0)
    z_step(3, 1)
    with scope("v2"):
        rs_v.second()
    z_block(2)
    with scope("q3"):
        rs_q.third()
    with scope("k2"):
        rs_k.second()
    z_step(2, 0)
    z_step(2, 1)
    z_block(1)
    with scope("v3"):
        rs_v.third()
    z_step(1, 0)
    with scope("k3"):
        rs_k.third()
    z_step(1, 1)
    last = input_block(z)
    with scope("q5"):
        rs_q.finish(dq_out)
        put(dq_out, dq_hbm, 0)
    with scope("v5"):
        rs_v.finish(dv_out)
        put(dv_out, dv_hbm, 2)
    with scope("zlast"):
        for copies in zs:
            for copy in copies:
                copy.wait_recv()
        dx_out[...] = (last + zr[0, 3].astype(F32) + zr[1, 3].astype(F32)).astype(BF16)
        put(dx_out, dx_hbm, 3)
    with scope("k5"):
        rs_k.finish(dk_out)
        put(dk_out, dk_hbm, 1)
    for copy in stored:
        copy.wait()
    for copy in started:
        copy.wait_send()


def publish(*refs):
    sources, targets, buffers, sem = refs[:4], refs[4:8], refs[8:12], refs[12]
    reads = [pltpu.make_async_copy(sources[i], buffers[i], sem.at[i]) for i in range(4)]
    writes = [pltpu.make_async_copy(buffers[i], targets[i], sem.at[4 + i]) for i in range(4)]
    for copy in reads:
        copy.start()
    for read, write in zip(reads, writes):
        read.wait()
        write.start()
    for copy in writes:
        copy.wait()


def body(normed, queries, keys, values, grads, links, wq, wk, wv):
    length, cols = queries.shape[2:]
    width = normed.shape[-1]
    heads = cols // HD
    rows = wq.shape[0]
    vmem = pl.BlockSpec(memory_space=pltpu.VMEM)
    anywhere = pl.BlockSpec(memory_space=pl.ANY)
    count = 176
    out = pl.pallas_call(
        kernel,
        out_shape=(
            jax.ShapeDtypeStruct((length, cols), BF16),
            jax.ShapeDtypeStruct((rows, cols), F32),
            jax.ShapeDtypeStruct((rows, cols), F32),
            jax.ShapeDtypeStruct((rows, cols), F32),
        ),
        in_specs=[pl.BlockSpec(memory_space=pltpu.SMEM)] + [anywhere] * 8,
        out_specs=(anywhere,) * 4,
        scratch_shapes=[
            pltpu.VMEM((length, cols), BF16),
            *[pltpu.VMEM((rows, cols), F32)] * 3,
            pltpu.VMEM((length, width), BF16),
            *[pltpu.VMEM((length, cols), BF16)] * 4,
            pltpu.VMEM((2, 2, heads, length, HD), BF16),
            pltpu.VMEM((2, 2, heads, length, HD), BF16),
            pltpu.VMEM((4, 2, 2, 2, rows, 3 * cols), BF16),
            pltpu.VMEM((4, 2, 2, 2, rows, length), BF16),
            pltpu.VMEM((4, 2, 2, rows, length), BF16),
            pltpu.VMEM((length, 3 * cols), BF16),
            pltpu.VMEM((length, 3 * cols), BF16),
            pltpu.VMEM((heads, 2, length, HD), F32),
            pltpu.VMEM((2, heads, 2, length, HD), BF16),
            pltpu.VMEM((2, heads, 2, length, HD), BF16),
            pltpu.VMEM((3, 4, 4, rows, cols), BF16),
            pltpu.VMEM((3, 2, 2, rows, cols), BF16),
            pltpu.VMEM((3, 2, 4, rows, cols), BF16),
            pltpu.VMEM((3, 4, rows, cols), BF16),
            pltpu.VMEM((3, 3, rows, cols), BF16),
            pltpu.VMEM((8, length, cols), BF16),
            pltpu.VMEM((2, 4, length, cols), BF16),
            pltpu.SemaphoreType.DMA((count,)),
            pltpu.SemaphoreType.DMA((count,)),
            pltpu.SemaphoreType.DMA((8,)),
        ],
        compiler_params=pltpu.CompilerParams(
            collective_id=0, has_side_effects=True, vmem_limit_bytes=56 * 1024 * 1024
        ),
        name="attention_backward",
    )(
        links,
        normed.reshape(length, width),
        *(value.reshape(length, cols) for value in (queries, keys, values, grads)),
        wq, wk, wv,
    )
    out = pl.pallas_call(
        publish,
        out_shape=[jax.ShapeDtypeStruct(o.shape, o.dtype) for o in out],
        in_specs=[anywhere] * 4,
        out_specs=[anywhere] * 4,
        scratch_shapes=[pltpu.VMEM(o.shape, o.dtype) for o in out] + [pltpu.SemaphoreType.DMA((8,))],
        name="publish",
    )(*out)
    return (out[0].reshape(1, 1, length, cols), out[1], out[2], out[3])


def solution(mesh):
    tokens = P("dp", "view", None, "head")
    weight = P(("dp", "view"), "head")
    return jax.shard_map(
        body,
        mesh=mesh,
        in_specs=(P("dp", "view", None, None),) + (tokens,) * 4 + (P("view", None),) + (weight,) * 3,
        out_specs=(tokens,) + (weight,) * 3,
        check_vma=False,
    )
```

```python
import contextlib

import jax
import jax.numpy as jnp
from jax import lax
from jax.experimental import pallas as pl
from jax.experimental.pallas import tpu as pltpu
from jax.sharding import PartitionSpec as P

HD = 128
SPLIT = 64
MESH = pl.DeviceIdType.MESH
F32 = jnp.float32
BF16 = jnp.bfloat16
NT = (((1,), (1,)), ((), ()))
NN = (((1,), (0,)), ((), ()))
TN = (((0,), (0,)), ((), ()))


def scope(name):
    return contextlib.nullcontext()


def dot(a, b, dims):
    return lax.dot_general(a, b, dims, preferred_element_type=F32)


def kernel(
    links, n_hbm, q_hbm, k_hbm, v_hbm, g_hbm, wq, wk, wv,
    dx_hbm, dq_hbm, dk_hbm, dv_hbm,
    dx_out, dq_out, dk_out, dv_out,
    normed, q_ref, k_ref, v_ref, g_ref,
    relay, kv, wg, nt, ntp, hown, hpar, own, gs, gr, part, ra1, rra, rb, rrb, zb, zr,
    ssem, rsem, lsem,
):
    length, cols = q_ref.shape
    heads = cols // HD
    rows = wq.shape[0]
    half = rows // 2
    scaling = HD ** (-0.5)
    dp, vw, z = lax.axis_index("dp"), lax.axis_index("view"), lax.axis_index("head")
    nz = 8
    x = lax.div(vw, 4)
    yh = lax.rem(lax.div(vw, 2), 2)
    c = lax.rem(vw, 2)
    y = yh * 2 + dp

    def at(xx, yy, cc, zz):
        return (lax.rem(yy, 2), xx * 4 + lax.div(yy, 2) * 2 + cc, zz)

    def m(value, n):
        return lax.rem(value + 2 * n, n)

    x_up, x_dn, x_far = m(x + 1, 4), m(x - 1, 4), m(x + 2, 4)
    y_up, y_dn = m(y + 1, 4), m(y - 1, 4)
    to_x = {1: at(x_up, y, c, z), -1: at(x_dn, y, c, z)}
    to_y = {1: at(x, y_up, c, z), -1: at(x, y_dn, c, z)}
    to_z = {1: (dp, vw, m(z + 1, nz)), -1: (dp, vw, m(z - 1, nz))}
    partner = at(x, y, 1 - c, z)

    def cross(yy):
        upper = lax.div(yy, 2)
        return c * upper - (1 - c) * (1 - upper)

    def outward(yy):
        return at(m(x + cross(yy), 4), m(yy + 2, 4), 1 - c, z)

    over = (outward(m(y - 1, 4)), outward(m(y + 1, 4)))

    started = []

    def send(src, dst, device):
        slot = len(started)
        copy = pltpu.make_async_remote_copy(
            src_ref=src, dst_ref=dst, send_sem=ssem.at[slot], recv_sem=rsem.at[slot],
            device_id=device, device_id_type=MESH,
        )
        copy.start()
        started.append(copy)
        return copy

    barrier = pltpu.get_barrier_semaphore()
    peers = [partner, at(x_far, y, c, z), at(x, m(y + 2, 4), c, z)]
    for ring in (to_x, to_y, to_z):
        peers += [ring[1], ring[-1]]
    peers += [at(m(x + cross(y), 4), m(y + s, 4), 1 - c, z) for s in (1, -1)]
    for peer in peers:
        pl.semaphore_signal(barrier, inc=1, device_id=peer, device_id_type=MESH)
    yl = dp

    def load(src, dst, slot):
        copy = pltpu.make_async_copy(src, dst, lsem.at[slot])
        copy.start()
        return copy

    stored = []

    def put(src, dst, slot):
        stored.append(load(src, dst, slot))

    w_loads = [
        load(w, wg.at[x, yl, yh, c, :, pl.ds(i * cols, cols)], i)
        for i, w in enumerate((wq, wk, wv))
    ]
    kv_loads = [load(k_hbm, k_ref, 3), load(v_hbm, v_ref, 4)]
    loads = [load(q_hbm, q_ref, 5), load(g_hbm, g_ref, 6), load(n_hbm, normed, 7)]
    for copy in w_loads + kv_loads:
        copy.wait()
    with scope("barrier"):
        pl.semaphore_wait(barrier, len(peers))

    class Gather:
        def __init__(self, start, size, x_first):
            self.x_first = x_first
            self.all = pl.ds(start, size)
            self.to_a, self.to_b = (to_x, to_y) if x_first else (to_y, to_x)
            self.half = (pl.ds(start, size // 2), pl.ds(start + size // 2, size // 2))
            self.b1, self.b2, self.par, self.tail = {}, {}, {}, []

        def ref(self, ao, bo, piece):
            xo, yo = (ao, bo) if self.x_first else (bo, ao)
            yy = m(y + yo, 4)
            return wg.at[m(x + xo, 4), lax.rem(yy, 2), lax.div(yy, 2), c, piece]

        def pass_on(self, ao, bo, piece, device):
            block = self.ref(ao, bo, piece)
            return send(block, block, device)

        def start(self):
            self.a1 = [self.pass_on(0, 0, self.all, self.to_a[s]) for s in (1, -1)]

        def across(self, ao):
            self.b1[ao] = [self.pass_on(ao, 0, self.all, self.to_b[s]) for s in (1, -1)]

        def forward(self):
            for copy in self.a1:
                copy.wait_recv()
            self.a2 = [self.pass_on(-s, 0, self.half[i], self.to_a[s]) for i, s in enumerate((1, -1))]

        def far(self):
            for copy in self.a2:
                copy.wait_recv()

        def across_forward(self, ao):
            for copy in self.b1[ao]:
                copy.wait_recv()
            self.b2[ao] = [self.pass_on(ao, -s, self.half[i], self.to_b[s]) for i, s in enumerate((1, -1))]

        def across_far(self, ao):
            for copy in self.b2[ao]:
                copy.wait_recv()
            self.tail.append(self.pass_on(ao, 2, self.all, partner))

        def to_partner(self, bo):
            if self.x_first:
                yy = m(y + bo, 4)
                block = wg.at[:, lax.rem(yy, 2), lax.div(yy, 2), c, self.all]
            else:
                block = wg.at[m(x + bo, 4), :, :, c, self.all]
            self.par[bo] = send(block, block, partner)

    ga = Gather(0, SPLIT, False)
    gb = Gather(SPLIT, rows - SPLIT, True)
    ga.start()
    gb.start()
    ga.across(0)
    halo, hops = [], []
    for h in range(heads):
        hs = pl.ds(h * HD, HD)
        pair = (k_ref.at[:, hs], v_ref.at[:, hs])
        halo.append([send(pair[i], kv.at[c, i, h], partner) for i in range(2)])
        hops.append([send(pair[i], relay.at[0, i, h], to_y[s]) for i, s in enumerate((1, -1))])
    for copy in loads:
        copy.wait()
    lo, hi = pl.ds(0, half), pl.ds(half, half)

    def transpose_chunk(i, _):
        chunk = normed[:, pl.ds(pl.multiple_of(i * 4 * rows, 128), 4 * rows)]
        turned = chunk.T.reshape(2, 2, rows, length)
        nt[lax.rem(i, 4), lax.div(i, 4)] = turned
        return 0

    with scope("transpose"):
        lax.fori_loop(0, 8, transpose_chunk, 0)
    with scope("gb_forward"):
        gb.forward()
    with scope("ga_forward"):
        ga.forward()
        ga.across(-1)
        ga.across(1)
    for h in range(heads):
        with scope("relay%d" % h):
            for i in range(2):
                hops[h][i].wait_recv()
                halo[h].append(send(relay.at[0, i, h], kv.at[1 - c, i, h], over[i]))
    gb.across(0)
    gb.across(-1)
    gb.across(1)
    turned_copy = send(nt.at[:, :, :, 1 - c], ntp, partner)
    with scope("ga_af0"):
        ga.across_forward(0)
    with scope("ga_far"):
        ga.far()
        ga.across(2)
        ga.to_partner(0)

    pen = [
        jnp.where(links[0, 0] >= 0, 0.0, -1e30).astype(F32),
        None,
        jnp.where(links[0, 1] >= 0, 0.0, -1e30).astype(F32),
    ]
    grad_halo, grad_hops = [], []
    w_x1, w_x2, w_par = [], [], []

    def attention(h):
        hs = slice(h * HD, (h + 1) * HD)
        for copy in halo[h]:
            copy.wait_recv()
        qh, gh = q_ref[:, hs], g_ref[:, hs]
        ks = [kv[0, 0, h], k_ref[:, hs], kv[1, 0, h]]
        vs = [kv[0, 1, h], v_ref[:, hs], kv[1, 1, h]]
        scores = []
        for j in range(3):
            s = dot(qh, ks[j], NT) * scaling
            scores.append(s if pen[j] is None else s + pen[j])
        top = jnp.maximum(jnp.maximum(scores[0], scores[1]), scores[2])
        top = jnp.max(top, axis=-1, keepdims=True)
        powers = [jnp.exp(s - top) for s in scores]
        total = jnp.sum(powers[0] + powers[1] + powers[2], axis=-1, keepdims=True)
        inv = 1.0 / total
        probs = [e * inv for e in powers]
        pgrads = [dot(gh, vj, NT) for vj in vs]
        delta = probs[0] * pgrads[0] + probs[1] * pgrads[1] + probs[2] * pgrads[2]
        delta = jnp.sum(delta, axis=-1, keepdims=True)
        sg = [(scaling * p * (d - delta)).astype(BF16) for p, d in zip(probs, pgrads)]
        query = dot(sg[0], ks[0], NN) + dot(sg[1], ks[1], NN) + dot(sg[2], ks[2], NN)
        hown[:, hs] = query.astype(BF16)
        for j, slot in ((0, 0), (2, 1)):
            gs[slot, h, 0] = dot(sg[j], qh, TN).astype(BF16)
            gs[slot, h, 1] = dot(probs[j].astype(BF16), gh, TN).astype(BF16)
        own[h, 0] = dot(sg[1], qh, TN)
        own[h, 1] = dot(probs[1].astype(BF16), gh, TN)
        grad_halo.append([send(gs.at[1 - c, h], gr.at[0, h], partner)])
        grad_hops.append(
            [send(gs.at[c, h, i], relay.at[1, i, h], to_y[s]) for i, s in enumerate((1, -1))]
        )

    def grad_relay(h):
        with scope("gr%d" % h):
            for i in range(2):
                grad_hops[h][i].wait_recv()
                grad_halo[h].append(send(relay.at[1, i, h], gr.at[1, h, i], over[i]))

    for h in range(heads):
        with scope("att"):
            attention(h)
    hq = hown.at[:, pl.ds(0, cols)]
    q_copy = send(hq, hpar.at[:, pl.ds(0, cols)], partner)
    with scope("ga_af1"):
        ga.across_forward(-1)
        ga.across_forward(1)
    grad_relay(0)
    grad_relay(1)
    with scope("gb_far"):
        gb.far()
        gb.across(2)
        gb.to_partner(0)

    def weight_part(first, *orders):
        cs = slice(first * cols, (first + len(orders)) * cols)

        def step(xx, _):
            a = nt[xx, :, :, c].reshape(4 * rows, length)
            b = ntp[xx].reshape(4 * rows, length)
            acc = dot(a, hown[:, cs], NN) + dot(b, hpar[:, cs], NN)
            acc = acc.astype(BF16)
            for i, x_first in enumerate(orders):
                for ll in range(2):
                    for hh in range(2):
                        yy, start = hh * 2 + ll, (ll * 2 + hh) * rows
                        block = acc[start : start + rows, i * cols : (i + 1) * cols]
                        if x_first:
                            part[first + i, xx, yy] = block
                        else:
                            part[first + i, yy, xx] = block
            return 0

        lax.fori_loop(0, 4, step, 0)

    class Scatter:
        def __init__(self, ci, pa, to_a, pb, to_b, to_far):
            self.ci, self.pa, self.to_a, self.pb, self.to_b = ci, pa, to_a, pb, to_b
            self.to_far = to_far
            self.aup, self.adn, self.afar = m(pa + 1, 4), m(pa - 1, 4), m(pa + 2, 4)
            self.bup, self.bdn, self.bfar = m(pb + 1, 4), m(pb - 1, 4), m(pb + 2, 4)

        def first(self):
            ci = self.ci
            low, high = pl.ds(0, 2), pl.ds(2, 2)
            self.f1 = [
                send(part.at[ci, self.afar, low], ra1.at[ci, 0], self.to_a[1]),
                send(part.at[ci, self.afar, high], ra1.at[ci, 1], self.to_a[-1]),
            ]
            self.f2 = [
                send(part.at[ci, self.aup, high], rra.at[ci, 0, high], self.to_a[1]),
                send(part.at[ci, self.adn, low], rra.at[ci, 1, low], self.to_a[-1]),
            ]

        def second(self):
            ci = self.ci
            low, high = pl.ds(0, 2), pl.ds(2, 2)
            for i, (block, piece, device) in enumerate(
                ((self.aup, low, self.to_a[1]), (self.adn, high, self.to_a[-1]))
            ):
                self.f1[i].wait_recv()
                old = part[ci, block, piece].astype(F32)
                part[ci, block, piece] = (old + ra1[ci, i].astype(F32)).astype(BF16)
                self.f2.append(send(part.at[ci, block, piece], rra.at[ci, i, piece], device))

        def third(self):
            ci = self.ci
            for copy in self.f2:
                copy.wait_recv()
            for j in range(4):
                value = part[ci, self.pa, j].astype(F32) + rra[ci, 0, j].astype(F32)
                rb[ci, j] = (value + rra[ci, 1, j].astype(F32)).astype(BF16)
            self.g2 = [
                send(rb.at[ci, self.bfar], rrb.at[ci, 2], self.to_far),
                send(rb.at[ci, self.bup], rrb.at[ci, 0], self.to_b[1]),
                send(rb.at[ci, self.bdn], rrb.at[ci, 1], self.to_b[-1]),
            ]

        def finish(self, out):
            ci = self.ci
            for copy in self.g2:
                copy.wait_recv()
            value = rb[ci, self.pb].astype(F32) + rrb[ci, 0].astype(F32)
            value = value + rrb[ci, 1].astype(F32) + rrb[ci, 2].astype(F32)
            out[...] = value * (1.0 / 32.0)

    y_far = at(x, m(y + 2, 4), c, z)
    rs_q = Scatter(0, x, to_x, y, to_y, y_far)
    rs_k = Scatter(1, x, to_x, y, to_y, y_far)
    rs_v = Scatter(2, y, to_y, x, to_x, at(x_far, y, c, z))

    with scope("wp_q"):
        turned_copy.wait_recv()
        q_copy.wait_recv()
        weight_part(0, True)
    grad_relay(2)
    with scope("ga_af2"):
        ga.across_forward(2)
        ga.to_partner(-1)
        ga.to_partner(1)
    rs_q.first()
    with scope("ga_bf0"):
        ga.across_far(0)
    with scope("gb_af1"):
        gb.across_forward(0)
        gb.across_forward(-1)
        gb.across_forward(1)
    with scope("gh_wait"):
        for h in range(heads):
            for copy in grad_halo[h]:
                copy.wait_recv()
            for i in range(2):
                value = own[h, i] + gr[0, h, i].astype(F32) + gr[1, h, i].astype(F32)
                start = (1 + i) * cols + h * HD
                hown[:, start : start + HD] = value.astype(BF16)
    hkv = pl.ds(cols, 2 * cols)
    kv_copy = send(hown.at[:, hkv], hpar.at[:, hkv], partner)
    with scope("gb_af2"):
        gb.across_forward(2)
        gb.to_partner(-1)
        gb.to_partner(1)
    with scope("ga_bf1"):
        ga.across_far(-1)
        ga.across_far(1)
    with scope("wp_v"):
        kv_copy.wait_recv()
        weight_part(1, True, False)
    rs_v.first()
    with scope("ga_bf"):
        ga.across_far(2)
    with scope("gb_bf"):
        for ao in (0, -1, 1, 2):
            gb.across_far(ao)
    with scope("q2"):
        rs_q.second()
    rs_k.first()
    with scope("wpar"):
        for group in (ga, gb):
            for copy in list(group.par.values()) + group.tail:
                copy.wait_recv()

    def input_block(j):
        w = wg[lax.rem(j, 4), lax.div(j, 4)].reshape(4 * rows, 3 * cols)
        return dot(hown[...], w, NT)

    part_rows = length // 2
    half_rows = part_rows // 2
    far = m(z + 4, nz)
    with scope("zfar"):
        zb[far] = input_block(far).astype(BF16)
    zs = [[], []]
    for p in range(2):
        for i, sign in ((0, 1), (1, -1)):
            piece = pl.ds(p * part_rows + i * half_rows, half_rows)
            zs[p].append(send(zb.at[far, piece], zr.at[i, 0, piece], to_z[sign]))

    def z_block(step):
        with scope("zb"):
            for sign in (1, -1):
                j = m(z + sign * step, nz)
                zb[j] = input_block(j).astype(BF16)

    def z_step(step, p):
        with scope("z%d%d" % (step, p)):
            new = []
            whole = pl.ds(p * part_rows, part_rows)
            for i, sign in ((0, 1), (1, -1)):
                piece = pl.ds(p * part_rows + i * half_rows, half_rows) if step == 3 else whole
                j = m(z + sign * step, nz)
                zs[p][i].wait_recv()
                value = zb[j, piece].astype(F32) + zr[i, 3 - step, piece].astype(F32)
                zb[j, piece] = value.astype(BF16)
                new.append(send(zb.at[j, whole], zr.at[i, 4 - step, whole], to_z[sign]))
            zs[p] = new

    z_block(3)
    z_block(2)
    z_step(3, 0)
    z_step(3, 1)
    with scope("v2"):
        rs_v.second()
    with scope("q3"):
        rs_q.third()
    with scope("k2"):
        rs_k.second()
    z_step(2, 0)
    z_step(2, 1)
    z_block(1)
    with scope("v3"):
        rs_v.third()
    z_step(1, 0)
    with scope("k3"):
        rs_k.third()
    z_step(1, 1)
    last = input_block(z)
    with scope("q5"):
        rs_q.finish(dq_out)
        put(dq_out, dq_hbm, 0)
    with scope("v5"):
        rs_v.finish(dv_out)
        put(dv_out, dv_hbm, 2)
    with scope("zlast"):
        for copies in zs:
            for copy in copies:
                copy.wait_recv()
        dx_out[...] = (last + zr[0, 3].astype(F32) + zr[1, 3].astype(F32)).astype(BF16)
        put(dx_out, dx_hbm, 3)
    with scope("k5"):
        rs_k.finish(dk_out)
        put(dk_out, dk_hbm, 1)
    for copy in stored:
        copy.wait()
    for copy in started:
        copy.wait_send()


def publish(*refs):
    sources, targets, buffers, sem = refs[:4], refs[4:8], refs[8:12], refs[12]
    reads = [pltpu.make_async_copy(sources[i], buffers[i], sem.at[i]) for i in range(4)]
    writes = [pltpu.make_async_copy(buffers[i], targets[i], sem.at[4 + i]) for i in range(4)]
    for copy in reads:
        copy.start()
    for read, write in zip(reads, writes):
        read.wait()
        write.start()
    for copy in writes:
        copy.wait()


def body(normed, queries, keys, values, grads, links, wq, wk, wv):
    length, cols = queries.shape[2:]
    width = normed.shape[-1]
    heads = cols // HD
    rows = wq.shape[0]
    vmem = pl.BlockSpec(memory_space=pltpu.VMEM)
    anywhere = pl.BlockSpec(memory_space=pl.ANY)
    count = 176
    out = pl.pallas_call(
        kernel,
        out_shape=(
            jax.ShapeDtypeStruct((length, cols), BF16),
            jax.ShapeDtypeStruct((rows, cols), F32),
            jax.ShapeDtypeStruct((rows, cols), F32),
            jax.ShapeDtypeStruct((rows, cols), F32),
        ),
        in_specs=[pl.BlockSpec(memory_space=pltpu.SMEM)] + [anywhere] * 8,
        out_specs=(anywhere,) * 4,
        scratch_shapes=[
            pltpu.VMEM((length, cols), BF16),
            *[pltpu.VMEM((rows, cols), F32)] * 3,
            pltpu.VMEM((length, width), BF16),
            *[pltpu.VMEM((length, cols), BF16)] * 4,
            pltpu.VMEM((2, 2, heads, length, HD), BF16),
            pltpu.VMEM((2, 2, heads, length, HD), BF16),
            pltpu.VMEM((4, 2, 2, 2, rows, 3 * cols), BF16),
            pltpu.VMEM((4, 2, 2, 2, rows, length), BF16),
            pltpu.VMEM((4, 2, 2, rows, length), BF16),
            pltpu.VMEM((length, 3 * cols), BF16),
            pltpu.VMEM((length, 3 * cols), BF16),
            pltpu.VMEM((heads, 2, length, HD), F32),
            pltpu.VMEM((2, heads, 2, length, HD), BF16),
            pltpu.VMEM((2, heads, 2, length, HD), BF16),
            pltpu.VMEM((3, 4, 4, rows, cols), BF16),
            pltpu.VMEM((3, 2, 2, rows, cols), BF16),
            pltpu.VMEM((3, 2, 4, rows, cols), BF16),
            pltpu.VMEM((3, 4, rows, cols), BF16),
            pltpu.VMEM((3, 3, rows, cols), BF16),
            pltpu.VMEM((8, length, cols), BF16),
            pltpu.VMEM((2, 4, length, cols), BF16),
            pltpu.SemaphoreType.DMA((count,)),
            pltpu.SemaphoreType.DMA((count,)),
            pltpu.SemaphoreType.DMA((8,)),
        ],
        compiler_params=pltpu.CompilerParams(
            collective_id=0, has_side_effects=True, vmem_limit_bytes=56 * 1024 * 1024
        ),
        name="attention_backward",
    )(
        links,
        normed.reshape(length, width),
        *(value.reshape(length, cols) for value in (queries, keys, values, grads)),
        wq, wk, wv,
    )
    out = pl.pallas_call(
        publish,
        out_shape=[jax.ShapeDtypeStruct(o.shape, o.dtype) for o in out],
        in_specs=[anywhere] * 4,
        out_specs=[anywhere] * 4,
        scratch_shapes=[pltpu.VMEM(o.shape, o.dtype) for o in out] + [pltpu.SemaphoreType.DMA((8,))],
        name="publish",
    )(*out)
    return (out[0].reshape(1, 1, length, cols), out[1], out[2], out[3])


def solution(mesh):
    tokens = P("dp", "view", None, "head")
    weight = P(("dp", "view"), "head")
    return jax.shard_map(
        body,
        mesh=mesh,
        in_specs=(P("dp", "view", None, None),) + (tokens,) * 4 + (P("view", None),) + (weight,) * 3,
        out_specs=(tokens,) + (weight,) * 3,
        check_vma=False,
    )
```

```python
import contextlib

import jax
import jax.numpy as jnp
from jax import lax
from jax.experimental import pallas as pl
from jax.experimental.pallas import tpu as pltpu
from jax.sharding import PartitionSpec as P

HD = 128
SPLIT = 64
MESH = pl.DeviceIdType.MESH
F32 = jnp.float32
BF16 = jnp.bfloat16
NT = (((1,), (1,)), ((), ()))
NN = (((1,), (0,)), ((), ()))
TN = (((0,), (0,)), ((), ()))


def scope(name):
    return contextlib.nullcontext()


def dot(a, b, dims):
    return lax.dot_general(a, b, dims, preferred_element_type=F32)


def kernel(
    links, n_hbm, q_hbm, k_hbm, v_hbm, g_hbm, wq, wk, wv,
    dx_hbm, dq_hbm, dk_hbm, dv_hbm,
    dx_out, dq_out, dk_out, dv_out,
    normed, q_ref, k_ref, v_ref, g_ref,
    relay, kv, wg, nt, ntp, hown, hpar, own, gs, gr, part, ra1, rra, rb, rrb, zb, zr,
    ssem, rsem, lsem,
):
    length, cols = q_ref.shape
    heads = cols // HD
    rows = wq.shape[0]
    half = rows // 2
    scaling = HD ** (-0.5)
    dp, vw, z = lax.axis_index("dp"), lax.axis_index("view"), lax.axis_index("head")
    nz = 8
    x = lax.div(vw, 4)
    yh = lax.rem(lax.div(vw, 2), 2)
    c = lax.rem(vw, 2)
    y = yh * 2 + dp

    def at(xx, yy, cc, zz):
        return (lax.rem(yy, 2), xx * 4 + lax.div(yy, 2) * 2 + cc, zz)

    def m(value, n):
        return lax.rem(value + 2 * n, n)

    x_up, x_dn, x_far = m(x + 1, 4), m(x - 1, 4), m(x + 2, 4)
    y_up, y_dn = m(y + 1, 4), m(y - 1, 4)
    to_x = {1: at(x_up, y, c, z), -1: at(x_dn, y, c, z)}
    to_y = {1: at(x, y_up, c, z), -1: at(x, y_dn, c, z)}
    to_z = {1: (dp, vw, m(z + 1, nz)), -1: (dp, vw, m(z - 1, nz))}
    partner = at(x, y, 1 - c, z)

    def cross(yy):
        upper = lax.div(yy, 2)
        return c * upper - (1 - c) * (1 - upper)

    def outward(yy):
        return at(m(x + cross(yy), 4), m(yy + 2, 4), 1 - c, z)

    over = (outward(m(y - 1, 4)), outward(m(y + 1, 4)))

    started = []

    def send(src, dst, device):
        slot = len(started)
        copy = pltpu.make_async_remote_copy(
            src_ref=src, dst_ref=dst, send_sem=ssem.at[slot], recv_sem=rsem.at[slot],
            device_id=device, device_id_type=MESH,
        )
        copy.start()
        started.append(copy)
        return copy

    barrier = pltpu.get_barrier_semaphore()
    peers = [partner, at(x_far, y, c, z), at(x, m(y + 2, 4), c, z)]
    for ring in (to_x, to_y, to_z):
        peers += [ring[1], ring[-1]]
    peers += [at(m(x + cross(y), 4), m(y + s, 4), 1 - c, z) for s in (1, -1)]
    for peer in peers:
        pl.semaphore_signal(barrier, inc=1, device_id=peer, device_id_type=MESH)
    yl = dp

    def load(src, dst, slot):
        copy = pltpu.make_async_copy(src, dst, lsem.at[slot])
        copy.start()
        return copy

    stored = []

    def put(src, dst, slot):
        stored.append(load(src, dst, slot))

    w_loads = [
        load(w, wg.at[x, yl, yh, c, :, pl.ds(i * cols, cols)], i)
        for i, w in enumerate((wq, wk, wv))
    ]
    kv_loads = [load(k_hbm, k_ref, 3), load(v_hbm, v_ref, 4)]
    loads = [load(q_hbm, q_ref, 5), load(g_hbm, g_ref, 6), load(n_hbm, normed, 7)]
    for copy in w_loads + kv_loads:
        copy.wait()
    with scope("barrier"):
        pl.semaphore_wait(barrier, len(peers))

    class Gather:
        def __init__(self, start, size, x_first):
            self.x_first = x_first
            self.all = pl.ds(start, size)
            self.to_a, self.to_b = (to_x, to_y) if x_first else (to_y, to_x)
            self.half = (pl.ds(start, size // 2), pl.ds(start + size // 2, size // 2))
            self.b1, self.b2, self.par, self.tail = {}, {}, {}, []

        def ref(self, ao, bo, piece):
            xo, yo = (ao, bo) if self.x_first else (bo, ao)
            yy = m(y + yo, 4)
            return wg.at[m(x + xo, 4), lax.rem(yy, 2), lax.div(yy, 2), c, piece]

        def pass_on(self, ao, bo, piece, device):
            block = self.ref(ao, bo, piece)
            return send(block, block, device)

        def start(self):
            self.a1 = [self.pass_on(0, 0, self.all, self.to_a[s]) for s in (1, -1)]

        def across(self, ao):
            self.b1[ao] = [self.pass_on(ao, 0, self.all, self.to_b[s]) for s in (1, -1)]

        def forward(self):
            for copy in self.a1:
                copy.wait_recv()
            self.a2 = [self.pass_on(-s, 0, self.half[i], self.to_a[s]) for i, s in enumerate((1, -1))]

        def far(self):
            for copy in self.a2:
                copy.wait_recv()

        def across_forward(self, ao):
            for copy in self.b1[ao]:
                copy.wait_recv()
            self.b2[ao] = [self.pass_on(ao, -s, self.half[i], self.to_b[s]) for i, s in enumerate((1, -1))]

        def across_far(self, ao):
            for copy in self.b2[ao]:
                copy.wait_recv()
            self.tail.append(self.pass_on(ao, 2, self.all, partner))

        def to_partner(self, bo):
            if self.x_first:
                yy = m(y + bo, 4)
                block = wg.at[:, lax.rem(yy, 2), lax.div(yy, 2), c, self.all]
            else:
                block = wg.at[m(x + bo, 4), :, :, c, self.all]
            self.par[bo] = send(block, block, partner)

    ga = Gather(0, SPLIT, False)
    gb = Gather(SPLIT, rows - SPLIT, True)
    ga.start()
    gb.start()
    ga.across(0)
    halo, hops = [], []
    for h in range(heads):
        hs = pl.ds(h * HD, HD)
        pair = (k_ref.at[:, hs], v_ref.at[:, hs])
        halo.append([send(pair[i], kv.at[c, i, h], partner) for i in range(2)])
        hops.append([send(pair[i], relay.at[0, i, h], to_y[s]) for i, s in enumerate((1, -1))])
    for copy in loads:
        copy.wait()
    lo, hi = pl.ds(0, half), pl.ds(half, half)

    def transpose_chunk(i, _):
        chunk = normed[:, pl.ds(pl.multiple_of(i * 4 * rows, 128), 4 * rows)]
        turned = chunk.T.reshape(2, 2, rows, length)
        nt[lax.rem(i, 4), lax.div(i, 4)] = turned
        return 0

    with scope("transpose"):
        lax.fori_loop(0, 8, transpose_chunk, 0)
    with scope("gb_forward"):
        gb.forward()
    with scope("ga_forward"):
        ga.forward()
        ga.across(-1)
        ga.across(1)
    for h in range(heads):
        with scope("relay%d" % h):
            for i in range(2):
                hops[h][i].wait_recv()
                halo[h].append(send(relay.at[0, i, h], kv.at[1 - c, i, h], over[i]))
    gb.across(0)
    gb.across(-1)
    gb.across(1)
    turned_copy = send(nt.at[:, :, :, 1 - c], ntp, partner)
    with scope("ga_af0"):
        ga.across_forward(0)
    with scope("ga_far"):
        ga.far()
        ga.across(2)
        ga.to_partner(0)

    pen = [
        jnp.where(links[0, 0] >= 0, 0.0, -1e30).astype(F32),
        None,
        jnp.where(links[0, 1] >= 0, 0.0, -1e30).astype(F32),
    ]
    grad_halo, grad_hops = [], []
    w_x1, w_x2, w_par = [], [], []

    def attention(h):
        hs = slice(h * HD, (h + 1) * HD)
        for copy in halo[h]:
            copy.wait_recv()
        qh, gh = q_ref[:, hs], g_ref[:, hs]
        ks = [kv[0, 0, h], k_ref[:, hs], kv[1, 0, h]]
        vs = [kv[0, 1, h], v_ref[:, hs], kv[1, 1, h]]
        scores = []
        for j in range(3):
            s = dot(qh, ks[j], NT) * scaling
            scores.append(s if pen[j] is None else s + pen[j])
        top = jnp.maximum(jnp.maximum(scores[0], scores[1]), scores[2])
        top = jnp.max(top, axis=-1, keepdims=True)
        powers = [jnp.exp(s - top) for s in scores]
        total = jnp.sum(powers[0] + powers[1] + powers[2], axis=-1, keepdims=True)
        inv = 1.0 / total
        probs = [e * inv for e in powers]
        pgrads = [dot(gh, vj, NT) for vj in vs]
        delta = probs[0] * pgrads[0] + probs[1] * pgrads[1] + probs[2] * pgrads[2]
        delta = jnp.sum(delta, axis=-1, keepdims=True)
        sg = [(scaling * p * (d - delta)).astype(BF16) for p, d in zip(probs, pgrads)]
        query = dot(sg[0], ks[0], NN) + dot(sg[1], ks[1], NN) + dot(sg[2], ks[2], NN)
        hown[:, hs] = query.astype(BF16)
        for j, slot in ((0, 0), (2, 1)):
            gs[slot, h, 0] = dot(sg[j], qh, TN).astype(BF16)
            gs[slot, h, 1] = dot(probs[j].astype(BF16), gh, TN).astype(BF16)
        own[h, 0] = dot(sg[1], qh, TN)
        own[h, 1] = dot(probs[1].astype(BF16), gh, TN)
        grad_halo.append([send(gs.at[1 - c, h], gr.at[0, h], partner)])
        grad_hops.append(
            [send(gs.at[c, h, i], relay.at[1, i, h], to_y[s]) for i, s in enumerate((1, -1))]
        )

    def grad_relay(h):
        with scope("gr%d" % h):
            for i in range(2):
                grad_hops[h][i].wait_recv()
                grad_halo[h].append(send(relay.at[1, i, h], gr.at[1, h, i], over[i]))

    for h in range(heads):
        with scope("att"):
            attention(h)
    hq = hown.at[:, pl.ds(0, cols)]
    q_copy = send(hq, hpar.at[:, pl.ds(0, cols)], partner)
    with scope("ga_af1"):
        ga.across_forward(-1)
        ga.across_forward(1)
    grad_relay(0)
    grad_relay(1)
    with scope("gb_far"):
        gb.far()
        gb.across(2)
        gb.to_partner(0)

    def weight_part(first, *orders):
        cs = slice(first * cols, (first + len(orders)) * cols)

        def step(xx, _):
            a = nt[xx, :, :, c].reshape(4 * rows, length)
            b = ntp[xx].reshape(4 * rows, length)
            acc = dot(a, hown[:, cs], NN) + dot(b, hpar[:, cs], NN)
            acc = acc.astype(BF16)
            for i, x_first in enumerate(orders):
                for ll in range(2):
                    for hh in range(2):
                        yy, start = hh * 2 + ll, (ll * 2 + hh) * rows
                        block = acc[start : start + rows, i * cols : (i + 1) * cols]
                        if x_first:
                            part[first + i, xx, yy] = block
                        else:
                            part[first + i, yy, xx] = block
            return 0

        lax.fori_loop(0, 4, step, 0)

    class Scatter:
        def __init__(self, ci, pa, to_a, pb, to_b, to_far):
            self.ci, self.pa, self.to_a, self.pb, self.to_b = ci, pa, to_a, pb, to_b
            self.to_far = to_far
            self.aup, self.adn, self.afar = m(pa + 1, 4), m(pa - 1, 4), m(pa + 2, 4)
            self.bup, self.bdn, self.bfar = m(pb + 1, 4), m(pb - 1, 4), m(pb + 2, 4)

        def first(self):
            ci = self.ci
            low, high = pl.ds(0, 2), pl.ds(2, 2)
            self.f1 = [
                send(part.at[ci, self.afar, low], ra1.at[ci, 0], self.to_a[1]),
                send(part.at[ci, self.afar, high], ra1.at[ci, 1], self.to_a[-1]),
            ]
            self.f2 = [
                send(part.at[ci, self.aup, high], rra.at[ci, 0, high], self.to_a[1]),
                send(part.at[ci, self.adn, low], rra.at[ci, 1, low], self.to_a[-1]),
            ]

        def second(self):
            ci = self.ci
            low, high = pl.ds(0, 2), pl.ds(2, 2)
            for i, (block, piece, device) in enumerate(
                ((self.aup, low, self.to_a[1]), (self.adn, high, self.to_a[-1]))
            ):
                self.f1[i].wait_recv()
                old = part[ci, block, piece].astype(F32)
                part[ci, block, piece] = (old + ra1[ci, i].astype(F32)).astype(BF16)
                self.f2.append(send(part.at[ci, block, piece], rra.at[ci, i, piece], device))

        def third(self):
            ci = self.ci
            for copy in self.f2:
                copy.wait_recv()
            for j in range(4):
                value = part[ci, self.pa, j].astype(F32) + rra[ci, 0, j].astype(F32)
                rb[ci, j] = (value + rra[ci, 1, j].astype(F32)).astype(BF16)
            self.g2 = [
                send(rb.at[ci, self.bfar], rrb.at[ci, 2], self.to_far),
                send(rb.at[ci, self.bup], rrb.at[ci, 0], self.to_b[1]),
                send(rb.at[ci, self.bdn], rrb.at[ci, 1], self.to_b[-1]),
            ]

        def finish(self, out):
            ci = self.ci
            for copy in self.g2:
                copy.wait_recv()
            value = rb[ci, self.pb].astype(F32) + rrb[ci, 0].astype(F32)
            value = value + rrb[ci, 1].astype(F32) + rrb[ci, 2].astype(F32)
            out[...] = value * (1.0 / 32.0)

    y_far = at(x, m(y + 2, 4), c, z)
    rs_q = Scatter(0, x, to_x, y, to_y, y_far)
    rs_k = Scatter(1, x, to_x, y, to_y, y_far)
    rs_v = Scatter(2, y, to_y, x, to_x, at(x_far, y, c, z))

    with scope("wp_q"):
        turned_copy.wait_recv()
        q_copy.wait_recv()
        weight_part(0, True)
    grad_relay(2)
    with scope("ga_af2"):
        ga.across_forward(2)
        ga.to_partner(-1)
        ga.to_partner(1)
    rs_q.first()
    with scope("ga_bf0"):
        ga.across_far(0)
    with scope("gb_af1"):
        gb.across_forward(0)
        gb.across_forward(-1)
        gb.across_forward(1)
    with scope("gh_wait"):
        for h in range(heads):
            for copy in grad_halo[h]:
                copy.wait_recv()
            for i in range(2):
                value = own[h, i] + gr[0, h, i].astype(F32) + gr[1, h, i].astype(F32)
                start = (1 + i) * cols + h * HD
                hown[:, start : start + HD] = value.astype(BF16)
    hkv = pl.ds(cols, 2 * cols)
    kv_copy = send(hown.at[:, hkv], hpar.at[:, hkv], partner)
    with scope("gb_af2"):
        gb.across_forward(2)
        gb.to_partner(-1)
        gb.to_partner(1)
    with scope("ga_bf1"):
        ga.across_far(-1)
        ga.across_far(1)
    with scope("wp_v"):
        kv_copy.wait_recv()
        weight_part(1, True, False)
    rs_v.first()
    with scope("ga_bf"):
        ga.across_far(2)
    with scope("gb_bf"):
        for ao in (0, -1, 1, 2):
            gb.across_far(ao)
    with scope("q2"):
        rs_q.second()
    rs_k.first()
    with scope("wpar"):
        for group in (ga, gb):
            for copy in list(group.par.values()) + group.tail:
                copy.wait_recv()

    def input_block(j):
        w = wg[lax.rem(j, 4), lax.div(j, 4)].reshape(4 * rows, 3 * cols)
        return dot(hown[...], w, NT)

    part_rows = length // 2
    half_rows = part_rows // 2
    far = m(z + 4, nz)
    with scope("zfar"):
        zb[far] = input_block(far).astype(BF16)
    zs = [[], []]
    for p in range(2):
        for i, sign in ((0, 1), (1, -1)):
            piece = pl.ds(p * part_rows + i * half_rows, half_rows)
            zs[p].append(send(zb.at[far, piece], zr.at[i, 0, piece], to_z[sign]))

    def z_block(step):
        with scope("zb"):
            for sign in (1, -1):
                j = m(z + sign * step, nz)
                zb[j] = input_block(j).astype(BF16)

    def z_step(step, p):
        with scope("z%d%d" % (step, p)):
            new = []
            whole = pl.ds(p * part_rows, part_rows)
            for i, sign in ((0, 1), (1, -1)):
                piece = pl.ds(p * part_rows + i * half_rows, half_rows) if step == 3 else whole
                j = m(z + sign * step, nz)
                zs[p][i].wait_recv()
                value = zb[j, piece].astype(F32) + zr[i, 3 - step, piece].astype(F32)
                zb[j, piece] = value.astype(BF16)
                new.append(send(zb.at[j, whole], zr.at[i, 4 - step, whole], to_z[sign]))
            zs[p] = new

    z_block(3)
    z_block(2)
    z_step(3, 0)
    z_step(3, 1)
    with scope("v2"):
        rs_v.second()
    with scope("q3"):
        rs_q.third()
    with scope("k2"):
        rs_k.second()
    z_block(1)
    z_step(2, 0)
    z_step(2, 1)
    with scope("v3"):
        rs_v.third()
    z_step(1, 0)
    with scope("k3"):
        rs_k.third()
    z_step(1, 1)
    last = input_block(z)
    with scope("q5"):
        rs_q.finish(dq_out)
        put(dq_out, dq_hbm, 0)
    with scope("v5"):
        rs_v.finish(dv_out)
        put(dv_out, dv_hbm, 2)
    with scope("zlast"):
        for copies in zs:
            for copy in copies:
                copy.wait_recv()
        dx_out[...] = (last + zr[0, 3].astype(F32) + zr[1, 3].astype(F32)).astype(BF16)
        put(dx_out, dx_hbm, 3)
    with scope("k5"):
        rs_k.finish(dk_out)
        put(dk_out, dk_hbm, 1)
    for copy in stored:
        copy.wait()
    for copy in started:
        copy.wait_send()


def publish(*refs):
    sources, targets, buffers, sem = refs[:4], refs[4:8], refs[8:12], refs[12]
    reads = [pltpu.make_async_copy(sources[i], buffers[i], sem.at[i]) for i in range(4)]
    writes = [pltpu.make_async_copy(buffers[i], targets[i], sem.at[4 + i]) for i in range(4)]
    for copy in reads:
        copy.start()
    for read, write in zip(reads, writes):
        read.wait()
        write.start()
    for copy in writes:
        copy.wait()


def body(normed, queries, keys, values, grads, links, wq, wk, wv):
    length, cols = queries.shape[2:]
    width = normed.shape[-1]
    heads = cols // HD
    rows = wq.shape[0]
    vmem = pl.BlockSpec(memory_space=pltpu.VMEM)
    anywhere = pl.BlockSpec(memory_space=pl.ANY)
    count = 176
    out = pl.pallas_call(
        kernel,
        out_shape=(
            jax.ShapeDtypeStruct((length, cols), BF16),
            jax.ShapeDtypeStruct((rows, cols), F32),
            jax.ShapeDtypeStruct((rows, cols), F32),
            jax.ShapeDtypeStruct((rows, cols), F32),
        ),
        in_specs=[pl.BlockSpec(memory_space=pltpu.SMEM)] + [anywhere] * 8,
        out_specs=(anywhere,) * 4,
        scratch_shapes=[
            pltpu.VMEM((length, cols), BF16),
            *[pltpu.VMEM((rows, cols), F32)] * 3,
            pltpu.VMEM((length, width), BF16),
            *[pltpu.VMEM((length, cols), BF16)] * 4,
            pltpu.VMEM((2, 2, heads, length, HD), BF16),
            pltpu.VMEM((2, 2, heads, length, HD), BF16),
            pltpu.VMEM((4, 2, 2, 2, rows, 3 * cols), BF16),
            pltpu.VMEM((4, 2, 2, 2, rows, length), BF16),
            pltpu.VMEM((4, 2, 2, rows, length), BF16),
            pltpu.VMEM((length, 3 * cols), BF16),
            pltpu.VMEM((length, 3 * cols), BF16),
            pltpu.VMEM((heads, 2, length, HD), F32),
            pltpu.VMEM((2, heads, 2, length, HD), BF16),
            pltpu.VMEM((2, heads, 2, length, HD), BF16),
            pltpu.VMEM((3, 4, 4, rows, cols), BF16),
            pltpu.VMEM((3, 2, 2, rows, cols), BF16),
            pltpu.VMEM((3, 2, 4, rows, cols), BF16),
            pltpu.VMEM((3, 4, rows, cols), BF16),
            pltpu.VMEM((3, 3, rows, cols), BF16),
            pltpu.VMEM((8, length, cols), BF16),
            pltpu.VMEM((2, 4, length, cols), BF16),
            pltpu.SemaphoreType.DMA((count,)),
            pltpu.SemaphoreType.DMA((count,)),
            pltpu.SemaphoreType.DMA((8,)),
        ],
        compiler_params=pltpu.CompilerParams(
            collective_id=0, has_side_effects=True, vmem_limit_bytes=56 * 1024 * 1024
        ),
        name="attention_backward",
    )(
        links,
        normed.reshape(length, width),
        *(value.reshape(length, cols) for value in (queries, keys, values, grads)),
        wq, wk, wv,
    )
    out = pl.pallas_call(
        publish,
        out_shape=[jax.ShapeDtypeStruct(o.shape, o.dtype) for o in out],
        in_specs=[anywhere] * 4,
        out_specs=[anywhere] * 4,
        scratch_shapes=[pltpu.VMEM(o.shape, o.dtype) for o in out] + [pltpu.SemaphoreType.DMA((8,))],
        name="publish",
    )(*out)
    return (out[0].reshape(1, 1, length, cols), out[1], out[2], out[3])


def solution(mesh):
    tokens = P("dp", "view", None, "head")
    weight = P(("dp", "view"), "head")
    return jax.shard_map(
        body,
        mesh=mesh,
        in_specs=(P("dp", "view", None, None),) + (tokens,) * 4 + (P("view", None),) + (weight,) * 3,
        out_specs=(tokens,) + (weight,) * 3,
        check_vma=False,
    )
```
